128 devices in a mesh: grp: 4 (over y), tile: 32 (over z, x, core).
Axes of the slice: x: 4, y: 4, z: 4, core: 2. Of those that a mesh axis runs over, the one named last changes fastest.
Arguments:
- tangents: float32 [2, 192, 256, 512], P(None, None, 'tile', 'grp'), may hold values from -60000 to 60000
- reaction_self: float32 [256, 512], P('tile', 'grp'), may hold values from -0.45 to -0.2
- reaction_cross: float32 [256, 512], P('tile', 'grp'), may hold values from -0.3 to -0.02
Outputs:
- corrections: float32 [24576, 192], P(('grp', 'tile'))
- growth: float32 [192], replicated
The draws below stay inside these ranges and needn't reach their ends.
All inputs are finite; a program needn't handle non-finite values.
Results may differ from the reference program's by a relative error of at most 0.0003.
Values sent between devices are 32-bit elements; how exact they have to be, the bound alone decides.
A program may use at most 64 MiB of HBM per device.

```python
import math
import jax
import jax.numpy as jnp
from jax import lax

K = 192
NYD = 8
NXD = 128
STEPS = 4
TILES = 32
BLOCKS = 128
NY = 256
NX = 512


def draw_tangents(key, part):
    subkeys = jax.random.split(key, 8)
    full_shape = (2, K, NY, NX)
    column_shape = (2, K, 1, NX)
    row_index = jnp.arange(NY, dtype=jnp.float32)[None, None, :, None]
    row_position = jnp.arange(NY, dtype=jnp.float32)[:, None] / NY
    column_position = jnp.arange(NX, dtype=jnp.float32)[None, :] / NX
    wavelength = 32.0 * jnp.exp(jax.random.uniform(subkeys[0], (1, K, 1, 1), jnp.float32) * math.log(4.0))
    phase = jax.random.uniform(subkeys[1], column_shape, jnp.float32, -math.pi, math.pi)
    offset = jax.random.truncated_normal(subkeys[2], -4.0, 4.0, column_shape, jnp.float32)
    amplitude = jax.random.truncated_normal(subkeys[3], -4.0, 4.0, column_shape, jnp.float32)
    noise = 0.25 * jax.random.truncated_normal(subkeys[4], -4.0, 4.0, full_shape, jnp.float32)
    trend_factor = 3.0 ** (row_position + column_position)
    smooth = offset + amplitude * jnp.cos(2.0 * math.pi * row_index / wavelength + phase)
    values = smooth + noise
    field_scale = jnp.array([1.0, 0.03], jnp.float32).reshape(2, 1, 1, 1)
    column_scale = jnp.exp(jax.random.uniform(subkeys[6], (1, K, 1, 1), jnp.float32) * math.log(10.0))
    cell_scale = jnp.exp(jax.random.uniform(subkeys[7], (1, 1, 1, NX), jnp.float32) * math.log(4.0))
    result = values * field_scale * column_scale * cell_scale * trend_factor
    return jnp.clip(result, -60000.0, 60000.0)


def block_levels(rng, dims, cuts, smallest, top_value):
    factor_of, own = 1.0, jax.random.fold_in(rng, 6)
    for dim, shards_of in cuts:
        draws = jnp.exp(jax.random.uniform(jax.random.fold_in(own, dim), (shards_of,), jnp.float32, smallest / len(cuts), top_value / len(cuts)))
        factor_of = factor_of * jnp.repeat(draws, dims[dim] // shards_of).reshape([-1 if axis == dim else 1 for axis in range(len(dims))])
    return factor_of


def setup_inputs(seed: int = 0) -> dict:
    keys = jax.random.split(jax.random.key(seed), 4)
    tangents = draw_tangents(jax.random.fold_in(keys[3], 71), 0)
    reaction_self = jnp.clip(-0.45 + 0.24999999 * jax.random.uniform(keys[1], (NY, NX), jnp.float32) ** block_levels(keys[1], (NY, NX), ((0, 32), (1, 4)), -0.2, 0.2), -0.45, -0.2)
    reaction_cross = jnp.clip(-0.3 + 0.28 * jax.random.uniform(keys[2], (NY, NX), jnp.float32) ** block_levels(keys[2], (NY, NX), ((0, 32), (1, 4)), -0.2, 0.2), -0.3, -0.02)
    return dict(tangents=tangents, reaction_self=reaction_self, reaction_cross=reaction_cross)


diffusion = 0.2
slow_rate = 0.05

def laplace(field):
    padded = jnp.pad(field, ((0, 0), (1, 1), (1, 1)), mode='edge')
    return padded[:, :-2, 1:-1] + padded[:, 2:, 1:-1] + padded[:, 1:-1, :-2] + padded[:, 1:-1, 2:] - 4.0 * field

def reference(tangents, reaction_self, reaction_cross):
    block_width = math.gcd(K, 32)
    block_count = K // block_width

    def evolve_block(column_block):
        start = column_block * block_width
        fast_field = lax.dynamic_slice_in_dim(tangents[0], start, block_width, 0)
        slow_field = lax.dynamic_slice_in_dim(tangents[1], start, block_width, 0)
        for repeat in range(STEPS):
            laplacian = laplace(fast_field)
            new_fast = fast_field + diffusion * laplacian + reaction_self * fast_field + reaction_cross * slow_field
            slow_field = slow_field + slow_rate * (fast_field - slow_field)
            fast_field = new_fast
        return jnp.stack([fast_field, slow_field])
    evolved = lax.map(evolve_block, jnp.arange(block_count, dtype=jnp.int32))

    def local_gram(block_index):
        group_index = block_index // TILES
        tile_index = block_index % TILES
        anchor = jnp.zeros((), jnp.int32)
        piece = lax.dynamic_slice(evolved, (anchor, anchor, anchor, (tile_index * NYD).astype(jnp.int32), (group_index * NXD).astype(jnp.int32)), (block_count, 2, block_width, NYD, NXD))
        piece = jnp.transpose(piece, (1, 0, 2, 3, 4)).reshape(2, K, NYD, NXD)
        return jnp.einsum('fkyx,fjyx->kj', piece, piece, precision=lax.Precision.HIGHEST)
    grams = lax.map(local_gram, jnp.arange(BLOCKS, dtype=jnp.int32))
    gram = lax.optimization_barrier(jnp.sum(grams, axis=0))
    factor = jnp.linalg.cholesky(gram)
    local_factors = jnp.linalg.cholesky(grams)

    def solve_block(local_factor):
        return jax.scipy.linalg.solve_triangular(factor, local_factor, lower=True)
    solved = lax.map(solve_block, local_factors)
    corrections = math.sqrt(BLOCKS) * jnp.transpose(solved, (0, 2, 1)).reshape(BLOCKS * K, K)
    growth = jnp.log(jnp.diagonal(factor))
    return (corrections, growth)
```

```python
import functools
import math

import jax
import jax.numpy as jnp
from jax import lax
from jax.experimental import pallas as pl
from jax.experimental.pallas import tpu as pltpu
from jax.sharding import PartitionSpec as P

MESH = pl.DeviceIdType.MESH
F32 = jnp.float32
STEPS = 4
K = 192
NYD = 8
LANES = 128
ROWS = K + 8
BLOCKS_K = ROWS // 8
CHUNKS = 5
CHUNK = ROWS // CHUNKS
PER_CHUNK = CHUNK // 8
EDGE = STEPS
EXT = NYD + 2 * EDGE
DIFFUSION = 0.2
SLOW_RATE = 0.05
VMEM_SPEC = pl.BlockSpec(memory_space=pltpu.VMEM)
NEIGHBOURS = [(dg, dt) for dg in (-1, 0, 1) for dt in (-1, 0, 1) if (dg, dt) != (0, 0)]


def lanes_of(shape=(8, LANES)):
    return lax.broadcasted_iota(jnp.int32, shape, 1)


def pack_kernel(tan_ref, self_ref, cross_ref, t_ref, left_ref, right_ref):
    lane = lanes_of()
    sub = lax.broadcasted_iota(jnp.int32, (8, LANES), 0)

    def body(fy, _):
        f = fy // NYD
        y = fy - f * NYD
        base = f * (K * NYD) + y
        own_self = jnp.broadcast_to(self_ref[pl.ds(y, 1), :], (8, LANES))
        own_cross = jnp.broadcast_to(cross_ref[pl.ds(y, 1), :], (8, LANES))
        block = jnp.where(sub == 0, own_self, own_cross)
        left = jnp.zeros((8, LANES), F32)
        right = jnp.zeros((8, LANES), F32)
        for b in range(BLOCKS_K):
            if b > 0:
                block = tan_ref[pl.ds(base + 64 * (b - 1), 8, stride=NYD), :]
            t_ref[fy, 8 * b : 8 * b + 8, :] = block
            here = (lane >= EDGE * b) & (lane < EDGE * b + EDGE)
            left = jnp.where(here, pltpu.roll(block, EDGE * b, 1) if b else block, left)
            right = jnp.where(here, pltpu.roll(block, (EDGE * b + EDGE) % LANES, 1), right)
        left_ref[fy] = left
        right_ref[fy] = right
        return 0

    lax.fori_loop(0, 2 * NYD, body, 0)


def pack(tangents, reaction_self, reaction_cross):
    return pl.pallas_call(
        pack_kernel,
        out_shape=(
            jax.ShapeDtypeStruct((2 * NYD, ROWS, LANES), F32),
            jax.ShapeDtypeStruct((2 * NYD, 8, LANES), F32),
            jax.ShapeDtypeStruct((2 * NYD, 8, LANES), F32),
        ),
        in_specs=[VMEM_SPEC] * 3,
        out_specs=[VMEM_SPEC] * 3,
        name="pack",
    )(tangents.reshape(2 * K * NYD, LANES), reaction_self, reaction_cross)


def stencil_kernel(
    groups, tiles,
    t_ref, left_ref, right_ref, e_ref,
    up_ref, down_ref, xl_ref, xr_ref, co_ref,
    row_send, row_recv, edge_send, edge_recv,
):
    g = lax.axis_index("grp")
    t = lax.axis_index("tile")
    has = {-1: t > 0, 0: None, 1: t < tiles - 1}
    hasg = {-1: g > 0, 0: None, 1: g < groups - 1}

    def exists(dg, dt):
        terms = [c for c in (hasg[dg], has[dt]) if c is not None]
        return terms[0] if len(terms) == 1 else terms[0] & terms[1]

    barrier = pltpu.get_barrier_semaphore()
    for dg, dt in NEIGHBOURS:
        @pl.when(exists(dg, dt))
        def _():
            pl.semaphore_signal(barrier, inc=1, device_id=(g + dg, t + dt), device_id_type=MESH)
    wide_g = 1 + (g > 0).astype(jnp.int32) + (g < groups - 1).astype(jnp.int32)
    wide_t = 1 + (t > 0).astype(jnp.int32) + (t < tiles - 1).astype(jnp.int32)
    pl.semaphore_wait(barrier, wide_g * wide_t - 1)

    def row_copies(direction, c):
        rows = pl.ds(pl.multiple_of(c * CHUNK, 8), CHUNK)
        if direction == 0:
            fast, slow, dst, dt = slice(0, 4), slice(8, 11), down_ref, -1
        else:
            fast, slow, dst, dt = slice(4, 8), slice(13, 16), up_ref, 1
        out = []
        for i, (src, where) in enumerate(((fast, slice(0, 4)), (slow, slice(4, 7)))):
            out.append(
                pltpu.make_async_remote_copy(
                    src_ref=t_ref.at[src, rows, :],
                    dst_ref=dst.at[where, rows, :],
                    send_sem=row_send.at[direction, c, i],
                    recv_sem=row_recv.at[direction, c, i],
                    device_id=(g, t + dt),
                    device_id_type=MESH,
                )
            )
        return out

    def edge_copies(side, dt):
        src = left_ref if side == 0 else right_ref
        dst = xr_ref if side == 0 else xl_ref
        dg = -1 if side == 0 else 1
        rows, where = {
            -1: (slice(0, 4), slice(12, 16)),
            0: (slice(0, 8), slice(4, 12)),
            1: (slice(4, 8), slice(0, 4)),
        }[dt]
        out = []
        for f in range(2):
            out.append(
                pltpu.make_async_remote_copy(
                    src_ref=src.at[slice(8 * f + rows.start, 8 * f + rows.stop)],
                    dst_ref=dst.at[slice(EXT * f + where.start, EXT * f + where.stop)],
                    send_sem=edge_send.at[side, dt + 1, f],
                    recv_sem=edge_recv.at[side, dt + 1, f],
                    device_id=(g + dg, t + dt),
                    device_id_type=MESH,
                )
            )
        return dg, out

    for direction, dt in ((0, -1), (1, 1)):
        @pl.when(has[dt])
        def _():
            for copy in row_copies(direction, 0):
                copy.start()
    for side in range(2):
        for dt in (0, -1, 1):
            dg, copies = edge_copies(side, dt)

            @pl.when(exists(dg, dt))
            def _():
                for copy in copies:
                    copy.start()
    for direction, dt in ((0, -1), (1, 1)):
        @pl.when(has[dt])
        def _():
            def start(c, _):
                for copy in row_copies(direction, c):
                    copy.start()
                return 0

            lax.fori_loop(1, CHUNKS, start, 0)

    def wait_rows(c):
        for direction, dt in ((0, 1), (1, -1)):
            @pl.when(has[dt])
            def _():
                for copy in row_copies(direction, c):
                    copy.wait_recv()

    for side in range(2):
        for dt in (0, -1, 1):
            dg, copies = edge_copies(side, dt)

            @pl.when(exists(-dg, -dt))
            def _():
                for copy in copies:
                    copy.wait_recv()

    wait_rows(0)

    lane = lanes_of()
    zero = jnp.zeros((8, LANES), jnp.int32)
    first_lane = lane == 0
    last_lane = lane == LANES - 1
    wall_left = first_lane & (zero + g == 0)
    wall_right = last_lane & (zero + g == groups - 1)
    wall_top = zero + t == 0
    wall_bottom = zero + t == tiles - 1
    near = lane < EDGE
    far = lane >= LANES - EDGE

    def main_of(f, e, b):
        rows = pl.ds(pl.multiple_of(8 * b, 8), 8)
        if e < EDGE:
            return up_ref[e if f == 0 else 4 + e - 1, rows, :]
        if e < EDGE + NYD:
            return t_ref[NYD * f + e - EDGE, rows, :]
        return down_ref[e - 12 + 4 * f, rows, :]

    def halo_of(f, e, b):
        to_low = lax.rem(LANES - EDGE * b, LANES)
        to_high = LANES - EDGE - EDGE * b
        from_right = pltpu.roll(xr_ref[EXT * f + e], to_low, 1)
        from_left = pltpu.roll(xl_ref[EXT * f + e], to_high, 1)
        return jnp.where(near, from_right, jnp.where(far, from_left, 0.0))

    for e in range(1, EXT - 1):
        for part, block in enumerate((main_of(0, e, 0), halo_of(0, e, jnp.int32(0)))):
            own = jnp.broadcast_to(block[0:1, :], (8, LANES)) + (1.0 - 4.0 * DIFFUSION)
            co_ref[part, 0, e] = own
            co_ref[part, 1, e] = jnp.broadcast_to(block[1:2, :], (8, LANES))

    def sides(value):
        main, halo = value
        lm, lh = pltpu.roll(main, 1, 1), pltpu.roll(halo, 1, 1)
        rm, rh = pltpu.roll(main, LANES - 1, 1), pltpu.roll(halo, LANES - 1, 1)
        left = jnp.where(wall_left, main, jnp.where(first_lane, lh, lm))
        right = jnp.where(wall_right, main, jnp.where(last_lane, rh, rm))
        return (
            left + right,
            jnp.where(first_lane, lm, lh) + jnp.where(last_lane, rm, rh),
        )

    def compute(b):
        fast = [[None] * EXT for _ in range(STEPS + 1)]
        slow = [[None] * EXT for _ in range(STEPS + 1)]
        for e in range(EXT):
            fast[0][e] = (main_of(0, e, b), halo_of(0, e, b))
            if 1 <= e < EXT - 1:
                slow[0][e] = (main_of(1, e, b), halo_of(1, e, b))
            for s in range(1, STEPS + 1):
                r = e - s
                if r < s or r > EXT - 1 - s:
                    continue
                old, old_slow = fast[s - 1][r], slow[s - 1][r]
                north, south = fast[s - 1][r - 1], fast[s - 1][r + 1]
                side = sides(old)
                new, new_slow = [], []
                for part in range(2 if s < STEPS else 1):
                    up, down = north[part], south[part]
                    if r == EDGE:
                        up = jnp.where(wall_top, old[part], up)
                    if r == EDGE + NYD - 1:
                        down = jnp.where(wall_bottom, old[part], down)
                    total = (up + down) + side[part]
                    new.append(
                        co_ref[part, 0, r] * old[part]
                        + DIFFUSION * total
                        + co_ref[part, 1, r] * old_slow[part]
                    )
                    new_slow.append(old_slow[part] + SLOW_RATE * (old[part] - old_slow[part]))
                fast[s][r] = tuple(new)
                slow[s][r] = tuple(new_slow)
                if s == STEPS:
                    rows = pl.ds(pl.multiple_of(8 * (b - 1), 8), 8)
                    e_ref[r - EDGE, rows, :] = new[0]
                    e_ref[NYD + r - EDGE, rows, :] = new_slow[0]

    def chunk(first, count):
        def body(i, _):
            compute(first + i)
            return 0

        lax.fori_loop(0, count, body, 0)

    chunk(1, PER_CHUNK - 1)

    def rest(c, _):
        wait_rows(c)
        chunk(c * PER_CHUNK, PER_CHUNK)
        return 0

    lax.fori_loop(1, CHUNKS, rest, 0)

    for direction, dt in ((0, -1), (1, 1)):
        @pl.when(has[dt])
        def _():
            def finish(c, _):
                for copy in row_copies(direction, c):
                    copy.wait_send()
                return 0

            lax.fori_loop(0, CHUNKS, finish, 0)
    for side in range(2):
        for dt in (0, -1, 1):
            dg, copies = edge_copies(side, dt)

            @pl.when(exists(dg, dt))
            def _():
                for copy in copies:
                    copy.wait_send()


def stencil(groups, tiles, packed, left, right):
    return pl.pallas_call(
        functools.partial(stencil_kernel, groups, tiles),
        out_shape=jax.ShapeDtypeStruct((2 * NYD, K, LANES), F32),
        in_specs=[VMEM_SPEC] * 3,
        out_specs=VMEM_SPEC,
        scratch_shapes=[
            pltpu.VMEM((7, ROWS, LANES), F32),
            pltpu.VMEM((7, ROWS, LANES), F32),
            pltpu.VMEM((2 * EXT, 8, LANES), F32),
            pltpu.VMEM((2 * EXT, 8, LANES), F32),
            pltpu.VMEM((2, 2, EXT, 8, LANES), F32),
            pltpu.SemaphoreType.DMA((2, CHUNKS, 2)),
            pltpu.SemaphoreType.DMA((2, CHUNKS, 2)),
            pltpu.SemaphoreType.DMA((2, 3, 2)),
            pltpu.SemaphoreType.DMA((2, 3, 2)),
        ],
        compiler_params=pltpu.CompilerParams(collective_id=0, has_side_effects=True),
        name="stencil",
    )(packed, left, right)


def gram_kernel(e_ref, g_ref, p_ref):
    total = jnp.zeros((K, K), F32)
    for i in range(2 * NYD):
        a = e_ref[i]
        total = total + lax.dot_general(
            a, a, (((1,), (1,)), ((), ())),
            precision=lax.Precision.HIGHEST, preferred_element_type=F32,
        )
    g_ref[...] = total
    zeros = jnp.zeros((64, 64), F32)
    p_ref[0:64, :] = total[0:64, 0:128]
    p_ref[64:128, :] = jnp.concatenate([total[0:64, 128:192], total[64:128, 64:128]], axis=1)
    p_ref[128:192, :] = jnp.concatenate([total[64:128, 128:192], total[128:192, 128:192]], axis=1)


def gram(evolved):
    return pl.pallas_call(
        gram_kernel,
        out_shape=(jax.ShapeDtypeStruct((K, K), F32), jax.ShapeDtypeStruct((K, LANES), F32)),
        in_specs=[VMEM_SPEC],
        out_specs=[VMEM_SPEC] * 2,
        name="gram",
    )(evolved)


def reduce_kernel(groups, tiles, p_ref, o_ref, near_ref, y_ref, z_ref, sends, recvs):
    g = lax.axis_index("grp")
    t = lax.axis_index("tile")
    inner = 8
    outer = tiles // inner
    piece = K // inner
    z = t // inner
    q = t - z * inner

    def in_line(d):
        return (g, z * inner + lax.rem(q + d, inner))

    def in_y(d):
        return (lax.rem(g + d, groups), t)

    def in_z(d):
        return (g, lax.rem(z + d, outer) * inner + q)

    peers = (
        [in_line(d) for d in range(1, inner)]
        + [in_y(d) for d in range(1, groups)]
        + [in_z(d) for d in range(1, outer)]
    )
    barrier = pltpu.get_barrier_semaphore()
    for peer in peers:
        pl.semaphore_signal(barrier, inc=1, device_id=peer, device_id_type=MESH)
    pl.semaphore_wait(barrier, len(peers))

    count = [0]

    def copy_to(src, dst, peer):
        i = count[0]
        count[0] += 1
        copy = pltpu.make_async_remote_copy(
            src_ref=src, dst_ref=dst, send_sem=sends.at[i], recv_sem=recvs.at[i],
            device_id=peer, device_id_type=MESH,
        )
        copy.start()
        return copy

    def rows(index):
        return pl.ds(pl.multiple_of(index * piece, 8), piece)

    started = []
    phase = []
    for d in range(1, inner):
        phase.append(copy_to(p_ref.at[rows(lax.rem(q + d, inner))], near_ref.at[d - 1], in_line(d)))
    total = p_ref[rows(q), :]
    for d, copy in enumerate(phase):
        copy.wait_recv()
        total = total + near_ref[d]
    started += phase
    for buf, me, size, peer_of in ((y_ref, g, groups, in_y), (z_ref, z, outer, in_z)):
        buf[me] = total
        phase = [copy_to(buf.at[me], buf.at[me], peer_of(d)) for d in range(1, size)]
        for copy in phase:
            copy.wait_recv()
        total = buf[0]
        for i in range(1, size):
            total = total + buf[i]
        started += phase
    o_ref[rows(q), :] = total
    phase = [copy_to(o_ref.at[rows(q)], o_ref.at[rows(q)], in_line(d)) for d in range(1, inner)]
    for copy in phase:
        copy.wait_recv()
    started += phase
    for copy in started:
        copy.wait_send()


def reduce_all(groups, tiles, packed):
    copies = 2 * 7 + (groups - 1) + (tiles // 8 - 1)
    return pl.pallas_call(
        functools.partial(reduce_kernel, groups, tiles),
        out_shape=jax.ShapeDtypeStruct((K, LANES), F32),
        in_specs=[VMEM_SPEC],
        out_specs=VMEM_SPEC,
        scratch_shapes=[
            pltpu.VMEM((7, K // 8, LANES), F32),
            pltpu.VMEM((groups, K // 8, LANES), F32),
            pltpu.VMEM((tiles // 8, K // 8, LANES), F32),
            pltpu.SemaphoreType.DMA((copies,)),
            pltpu.SemaphoreType.DMA((copies,)),
        ],
        compiler_params=pltpu.CompilerParams(collective_id=1, has_side_effects=True),
        name="reduce",
    )(packed)


def unpack(p):
    upper = jnp.zeros((K, K), F32)
    upper = upper.at[0:64, 0:128].set(p[0:64])
    upper = upper.at[0:64, 128:192].set(p[64:128, 0:64])
    upper = upper.at[64:128, 64:128].set(p[64:128, 64:128])
    upper = upper.at[64:128, 128:192].set(p[128:192, 0:64])
    upper = upper.at[128:192, 128:192].set(p[128:192, 64:128])
    upper = jnp.triu(upper)
    return upper + jnp.triu(upper, 1).T


def per_device(groups, tiles, tangents, reaction_self, reaction_cross):
    packed, left, right = pack(tangents, reaction_self, reaction_cross)
    evolved = stencil(groups, tiles, packed, left, right)
    local_gram, local_packed = gram(evolved)
    local_factor = jnp.linalg.cholesky(local_gram)
    total = unpack(reduce_all(groups, tiles, local_packed))
    factor = jnp.linalg.cholesky(total)
    solved = jax.scipy.linalg.solve_triangular(factor, local_factor, lower=True)
    corrections = math.sqrt(groups * tiles) * solved.T
    growth = jnp.log(jnp.diagonal(factor))
    return (corrections, growth)


def solution(mesh):
    groups, tiles = mesh.shape["grp"], mesh.shape["tile"]
    in_specs = (P(None, None, "tile", "grp"), P("tile", "grp"), P("tile", "grp"))
    out_specs = (P(("grp", "tile"), None), P())
    return jax.shard_map(
        functools.partial(per_device, groups, tiles),
        mesh=mesh, in_specs=in_specs, out_specs=out_specs, check_vma=False,
    )
```

```python
import functools
import math

import jax
import jax.numpy as jnp
from jax import lax
from jax.experimental import pallas as pl
from jax.experimental.pallas import tpu as pltpu
from jax.sharding import PartitionSpec as P

MESH = pl.DeviceIdType.MESH
F32 = jnp.float32
STEPS = 4
K = 192
NYD = 8
LANES = 128
ROWS = K + 8
BLOCKS_K = ROWS // 8
CHUNKS = 5
CHUNK = ROWS // CHUNKS
PER_CHUNK = CHUNK // 8
EDGE = STEPS
EXT = NYD + 2 * EDGE
DIFFUSION = 0.2
SLOW_RATE = 0.05
VMEM_SPEC = pl.BlockSpec(memory_space=pltpu.VMEM)
NEIGHBOURS = [(dg, dt) for dg in (-1, 0, 1) for dt in (-1, 0, 1) if (dg, dt) != (0, 0)]


def lanes_of(shape=(8, LANES)):
    return lax.broadcasted_iota(jnp.int32, shape, 1)


def pack_kernel(tan_ref, self_ref, cross_ref, t_ref, left_ref, right_ref):
    lane = lanes_of()
    sub = lax.broadcasted_iota(jnp.int32, (8, LANES), 0)

    def body(fy, _):
        f = fy // NYD
        y = fy - f * NYD
        base = f * (K * NYD) + y
        own_self = jnp.broadcast_to(self_ref[pl.ds(y, 1), :], (8, LANES))
        own_cross = jnp.broadcast_to(cross_ref[pl.ds(y, 1), :], (8, LANES))
        block = jnp.where(sub == 0, own_self, own_cross)
        left = jnp.zeros((8, LANES), F32)
        right = jnp.zeros((8, LANES), F32)
        for b in range(BLOCKS_K):
            if b > 0:
                block = tan_ref[pl.ds(base + 64 * (b - 1), 8, stride=NYD), :]
            t_ref[fy, 8 * b : 8 * b + 8, :] = block
            here = (lane >= EDGE * b) & (lane < EDGE * b + EDGE)
            left = jnp.where(here, pltpu.roll(block, EDGE * b, 1) if b else block, left)
            right = jnp.where(here, pltpu.roll(block, (EDGE * b + EDGE) % LANES, 1), right)
        left_ref[fy] = left
        right_ref[fy] = right
        return 0

    lax.fori_loop(0, 2 * NYD, body, 0)


def pack(tangents, reaction_self, reaction_cross):
    return pl.pallas_call(
        pack_kernel,
        out_shape=(
            jax.ShapeDtypeStruct((2 * NYD, ROWS, LANES), F32),
            jax.ShapeDtypeStruct((2 * NYD, 8, LANES), F32),
            jax.ShapeDtypeStruct((2 * NYD, 8, LANES), F32),
        ),
        in_specs=[VMEM_SPEC] * 3,
        out_specs=[VMEM_SPEC] * 3,
        name="pack",
    )(tangents.reshape(2 * K * NYD, LANES), reaction_self, reaction_cross)


def stencil_kernel(
    groups, tiles,
    t_ref, left_ref, right_ref, e_ref,
    up_ref, down_ref, xl_ref, xr_ref, co_ref,
    row_send, row_recv, edge_send, edge_recv,
):
    g = lax.axis_index("grp")
    t = lax.axis_index("tile")
    has = {-1: t > 0, 0: None, 1: t < tiles - 1}
    hasg = {-1: g > 0, 0: None, 1: g < groups - 1}

    def exists(dg, dt):
        terms = [c for c in (hasg[dg], has[dt]) if c is not None]
        return terms[0] if len(terms) == 1 else terms[0] & terms[1]

    barrier = pltpu.get_barrier_semaphore()
    for dg, dt in NEIGHBOURS:
        @pl.when(exists(dg, dt))
        def _():
            pl.semaphore_signal(barrier, inc=1, device_id=(g + dg, t + dt), device_id_type=MESH)
    wide_g = 1 + (g > 0).astype(jnp.int32) + (g < groups - 1).astype(jnp.int32)
    wide_t = 1 + (t > 0).astype(jnp.int32) + (t < tiles - 1).astype(jnp.int32)
    pl.semaphore_wait(barrier, wide_g * wide_t - 1)

    def row_copies(direction, c):
        rows = pl.ds(pl.multiple_of(c * CHUNK, 8), CHUNK)
        if direction == 0:
            fast, slow, dst, dt = slice(0, 4), slice(8, 11), down_ref, -1
        else:
            fast, slow, dst, dt = slice(4, 8), slice(13, 16), up_ref, 1
        out = []
        for i, (src, where) in enumerate(((fast, slice(0, 4)), (slow, slice(4, 7)))):
            out.append(
                pltpu.make_async_remote_copy(
                    src_ref=t_ref.at[src, rows, :],
                    dst_ref=dst.at[where, rows, :],
                    send_sem=row_send.at[direction, c, i],
                    recv_sem=row_recv.at[direction, c, i],
                    device_id=(g, t + dt),
                    device_id_type=MESH,
                )
            )
        return out

    def edge_copies(side, dt):
        src = left_ref if side == 0 else right_ref
        dst = xr_ref if side == 0 else xl_ref
        dg = -1 if side == 0 else 1
        rows, where = {
            -1: (slice(0, 4), slice(12, 16)),
            0: (slice(0, 8), slice(4, 12)),
            1: (slice(4, 8), slice(0, 4)),
        }[dt]
        out = []
        for f in range(2):
            out.append(
                pltpu.make_async_remote_copy(
                    src_ref=src.at[slice(8 * f + rows.start, 8 * f + rows.stop)],
                    dst_ref=dst.at[slice(EXT * f + where.start, EXT * f + where.stop)],
                    send_sem=edge_send.at[side, dt + 1, f],
                    recv_sem=edge_recv.at[side, dt + 1, f],
                    device_id=(g + dg, t + dt),
                    device_id_type=MESH,
                )
            )
        return dg, out

    for direction, dt in ((0, -1), (1, 1)):
        @pl.when(has[dt])
        def _():
            for copy in row_copies(direction, 0):
                copy.start()
    for side in range(2):
        for dt in (0, -1, 1):
            dg, copies = edge_copies(side, dt)

            @pl.when(exists(dg, dt))
            def _():
                for copy in copies:
                    copy.start()
    for direction, dt in ((0, -1), (1, 1)):
        @pl.when(has[dt])
        def _():
            def start(c, _):
                for copy in row_copies(direction, c):
                    copy.start()
                return 0

            lax.fori_loop(1, CHUNKS, start, 0)

    def wait_rows(c):
        for direction, dt in ((0, 1), (1, -1)):
            @pl.when(has[dt])
            def _():
                for copy in row_copies(direction, c):
                    copy.wait_recv()

    for side in range(2):
        for dt in (0, -1, 1):
            dg, copies = edge_copies(side, dt)

            @pl.when(exists(-dg, -dt))
            def _():
                for copy in copies:
                    copy.wait_recv()

    wait_rows(0)

    lane = lanes_of()
    zero = jnp.zeros((8, LANES), jnp.int32)
    first_lane = lane == 0
    last_lane = lane == LANES - 1
    wall_left = first_lane & (zero + g == 0)
    wall_right = last_lane & (zero + g == groups - 1)
    wall_top = zero + t == 0
    wall_bottom = zero + t == tiles - 1
    near = lane < EDGE
    far = lane >= LANES - EDGE

    def main_of(f, e, b):
        rows = pl.ds(pl.multiple_of(8 * b, 8), 8)
        if e < EDGE:
            return up_ref[e if f == 0 else 4 + e - 1, rows, :]
        if e < EDGE + NYD:
            return t_ref[NYD * f + e - EDGE, rows, :]
        return down_ref[e - 12 + 4 * f, rows, :]

    def halo_of(f, e, b):
        to_low = lax.rem(LANES - EDGE * b, LANES)
        to_high = LANES - EDGE - EDGE * b
        from_right = pltpu.roll(xr_ref[EXT * f + e], to_low, 1)
        from_left = pltpu.roll(xl_ref[EXT * f + e], to_high, 1)
        return jnp.where(near, from_right, jnp.where(far, from_left, 0.0))

    for e in range(1, EXT - 1):
        for part, block in enumerate((main_of(0, e, 0), halo_of(0, e, jnp.int32(0)))):
            own = jnp.broadcast_to(block[0:1, :], (8, LANES)) + (1.0 - 4.0 * DIFFUSION)
            co_ref[part, 0, e] = own
            co_ref[part, 1, e] = jnp.broadcast_to(block[1:2, :], (8, LANES))

    def sides(value):
        main, halo = value
        lm, lh = pltpu.roll(main, 1, 1), pltpu.roll(halo, 1, 1)
        rm, rh = pltpu.roll(main, LANES - 1, 1), pltpu.roll(halo, LANES - 1, 1)
        left = jnp.where(wall_left, main, jnp.where(first_lane, lh, lm))
        right = jnp.where(wall_right, main, jnp.where(last_lane, rh, rm))
        return (
            left + right,
            jnp.where(first_lane, lm, lh) + jnp.where(last_lane, rm, rh),
        )

    def compute(b):
        fast = [[None] * EXT for _ in range(STEPS + 1)]
        slow = [[None] * EXT for _ in range(STEPS + 1)]
        for e in range(EXT):
            fast[0][e] = (main_of(0, e, b), halo_of(0, e, b))
            if 1 <= e < EXT - 1:
                slow[0][e] = (main_of(1, e, b), halo_of(1, e, b))
            for s in range(1, STEPS + 1):
                r = e - s
                if r < s or r > EXT - 1 - s:
                    continue
                old, old_slow = fast[s - 1][r], slow[s - 1][r]
                north, south = fast[s - 1][r - 1], fast[s - 1][r + 1]
                side = sides(old)
                new, new_slow = [], []
                for part in range(2 if s < STEPS else 1):
                    up, down = north[part], south[part]
                    if r == EDGE:
                        up = jnp.where(wall_top, old[part], up)
                    if r == EDGE + NYD - 1:
                        down = jnp.where(wall_bottom, old[part], down)
                    total = (up + down) + side[part]
                    new.append(
                        co_ref[part, 0, r] * old[part]
                        + DIFFUSION * total
                        + co_ref[part, 1, r] * old_slow[part]
                    )
                    new_slow.append(old_slow[part] + SLOW_RATE * (old[part] - old_slow[part]))
                fast[s][r] = tuple(new)
                slow[s][r] = tuple(new_slow)
                if s == STEPS:
                    rows = pl.ds(pl.multiple_of(8 * (b - 1), 8), 8)
                    e_ref[r - EDGE, rows, :] = new[0]
                    e_ref[NYD + r - EDGE, rows, :] = new_slow[0]

    def chunk(first, count):
        def body(i, _):
            compute(first + i)
            return 0

        lax.fori_loop(0, count, body, 0)

    chunk(1, PER_CHUNK - 1)

    def rest(c, _):
        wait_rows(c)
        chunk(c * PER_CHUNK, PER_CHUNK)
        return 0

    lax.fori_loop(1, CHUNKS, rest, 0)

    for direction, dt in ((0, -1), (1, 1)):
        @pl.when(has[dt])
        def _():
            def finish(c, _):
                for copy in row_copies(direction, c):
                    copy.wait_send()
                return 0

            lax.fori_loop(0, CHUNKS, finish, 0)
    for side in range(2):
        for dt in (0, -1, 1):
            dg, copies = edge_copies(side, dt)

            @pl.when(exists(dg, dt))
            def _():
                for copy in copies:
                    copy.wait_send()


def stencil(groups, tiles, packed, left, right):
    return pl.pallas_call(
        functools.partial(stencil_kernel, groups, tiles),
        out_shape=jax.ShapeDtypeStruct((2 * NYD, K, LANES), F32),
        in_specs=[VMEM_SPEC] * 3,
        out_specs=VMEM_SPEC,
        scratch_shapes=[
            pltpu.VMEM((7, ROWS, LANES), F32),
            pltpu.VMEM((7, ROWS, LANES), F32),
            pltpu.VMEM((2 * EXT, 8, LANES), F32),
            pltpu.VMEM((2 * EXT, 8, LANES), F32),
            pltpu.VMEM((2, 2, EXT, 8, LANES), F32),
            pltpu.SemaphoreType.DMA((2, CHUNKS, 2)),
            pltpu.SemaphoreType.DMA((2, CHUNKS, 2)),
            pltpu.SemaphoreType.DMA((2, 3, 2)),
            pltpu.SemaphoreType.DMA((2, 3, 2)),
        ],
        compiler_params=pltpu.CompilerParams(collective_id=0, has_side_effects=True),
        name="stencil",
    )(packed, left, right)


def gram_kernel(e_ref, g_ref, p_ref):
    total = jnp.zeros((K, K), F32)
    for i in range(NYD):
        a = jnp.concatenate([e_ref[i], e_ref[NYD + i]], axis=1)
        total = total + lax.dot_general(
            a, a, (((1,), (1,)), ((), ())),
            precision=lax.Precision.HIGHEST, preferred_element_type=F32,
        )
    g_ref[...] = total
    zeros = jnp.zeros((64, 64), F32)
    p_ref[0:64, :] = total[0:64, 0:128]
    p_ref[64:128, :] = jnp.concatenate([total[0:64, 128:192], total[64:128, 64:128]], axis=1)
    p_ref[128:192, :] = jnp.concatenate([total[64:128, 128:192], total[128:192, 128:192]], axis=1)


def gram(evolved):
    return pl.pallas_call(
        gram_kernel,
        out_shape=(jax.ShapeDtypeStruct((K, K), F32), jax.ShapeDtypeStruct((K, LANES), F32)),
        in_specs=[VMEM_SPEC],
        out_specs=[VMEM_SPEC] * 2,
        name="gram",
    )(evolved)


def reduce_kernel(groups, tiles, p_ref, o_ref, near_ref, y_ref, z_ref, sends, recvs):
    g = lax.axis_index("grp")
    t = lax.axis_index("tile")
    inner = 8
    outer = tiles // inner
    piece = K // inner
    z = t // inner
    q = t - z * inner

    def in_line(d):
        return (g, z * inner + lax.rem(q + d, inner))

    def in_y(d):
        return (lax.rem(g + d, groups), t)

    def in_z(d):
        return (g, lax.rem(z + d, outer) * inner + q)

    peers = (
        [in_line(d) for d in range(1, inner)]
        + [in_y(d) for d in range(1, groups)]
        + [in_z(d) for d in range(1, outer)]
    )
    barrier = pltpu.get_barrier_semaphore()
    for peer in peers:
        pl.semaphore_signal(barrier, inc=1, device_id=peer, device_id_type=MESH)
    pl.semaphore_wait(barrier, len(peers))

    count = [0]

    def copy_to(src, dst, peer):
        i = count[0]
        count[0] += 1
        copy = pltpu.make_async_remote_copy(
            src_ref=src, dst_ref=dst, send_sem=sends.at[i], recv_sem=recvs.at[i],
            device_id=peer, device_id_type=MESH,
        )
        copy.start()
        return copy

    def rows(index):
        return pl.ds(pl.multiple_of(index * piece, 8), piece)

    started = []
    phase = []
    for d in range(1, inner):
        phase.append(copy_to(p_ref.at[rows(lax.rem(q + d, inner))], near_ref.at[d - 1], in_line(d)))
    total = p_ref[rows(q), :]
    for d, copy in enumerate(phase):
        copy.wait_recv()
        total = total + near_ref[d]
    started += phase
    for buf, me, size, peer_of in ((y_ref, g, groups, in_y), (z_ref, z, outer, in_z)):
        buf[me] = total
        phase = [copy_to(buf.at[me], buf.at[me], peer_of(d)) for d in range(1, size)]
        for copy in phase:
            copy.wait_recv()
        total = buf[0]
        for i in range(1, size):
            total = total + buf[i]
        started += phase
    o_ref[rows(q), :] = total
    phase = [copy_to(o_ref.at[rows(q)], o_ref.at[rows(q)], in_line(d)) for d in range(1, inner)]
    for copy in phase:
        copy.wait_recv()
    started += phase
    for copy in started:
        copy.wait_send()


def reduce_all(groups, tiles, packed):
    copies = 2 * 7 + (groups - 1) + (tiles // 8 - 1)
    return pl.pallas_call(
        functools.partial(reduce_kernel, groups, tiles),
        out_shape=jax.ShapeDtypeStruct((K, LANES), F32),
        in_specs=[VMEM_SPEC],
        out_specs=VMEM_SPEC,
        scratch_shapes=[
            pltpu.VMEM((7, K // 8, LANES), F32),
            pltpu.VMEM((groups, K // 8, LANES), F32),
            pltpu.VMEM((tiles // 8, K // 8, LANES), F32),
            pltpu.SemaphoreType.DMA((copies,)),
            pltpu.SemaphoreType.DMA((copies,)),
        ],
        compiler_params=pltpu.CompilerParams(collective_id=1, has_side_effects=True),
        name="reduce",
    )(packed)


def eliminate(w_ref, emit, invert):
    lane = lanes_of()
    sub = lax.broadcasted_iota(jnp.int32, (8, LANES), 0)
    panels = K // 8
    for p in range(panels):
        j0 = 8 * p
        h, l0 = j0 // LANES, j0 % LANES
        halves = (0, 1) if invert else tuple(range(h, 2))
        inside = (lane >= l0) & (lane < l0 + 8)
        blk = {v: w_ref[j0 : j0 + 8, LANES * v : LANES * v + LANES] for v in halves}
        cols = [jnp.broadcast_to(blk[h][:, l0 + i : l0 + i + 1], (8, LANES)) for i in range(8)]
        el = [
            [jnp.broadcast_to(cols[i][m : m + 1, :], (8, LANES)) if m >= i else None for i in range(8)]
            for m in range(8)
        ]
        if invert:
            blk[h] = jnp.where(inside, jnp.where(lane - l0 == sub, 1.0, 0.0), blk[h])
        rows = {v: [jnp.broadcast_to(blk[v][m : m + 1, :], (8, LANES)) for m in range(8)] for v in halves}
        fac = [[None] * 8 for _ in range(8)]
        r, r2, pivots = [], [], []
        for i in range(8):
            pivots.append(el[i][i])
            r.append(lax.rsqrt(el[i][i]))
            r2.append(r[i] * r[i])
            for m in range(i + 1, 8):
                fac[m][i] = el[m][i] * r2[i]
            for k in range(i + 1, 8):
                for m in range(k, 8):
                    el[m][k] = el[m][k] - fac[k][i] * el[m][i]
            for v in halves:
                for m in range(i + 1, 8):
                    rows[v][m] = rows[v][m] - fac[m][i] * rows[v][i]
        for v in halves:
            out = rows[v][0] * r[0]
            for i in range(1, 8):
                out = jnp.where(sub == i, rows[v][i] * r[i], out)
            emit(p, v, out, lane, sub)
        emit(p, None, pivots, lane, sub)
        if p == panels - 1:
            break
        z = {v: [None] * 8 for v in halves}
        for v in halves:
            for i in range(7, -1, -1):
                acc = rows[v][i] * r2[i]
                for m in range(7, i, -1):
                    acc = acc - fac[m][i] * z[v][m]
                z[v][i] = acc
        for s in range(p + 1, panels):
            rng = slice(8 * s, 8 * s + 8)
            src = w_ref[rng, LANES * h : LANES * h + LANES]
            low = [jnp.broadcast_to(src[:, l0 + i : l0 + i + 1], (8, LANES)) for i in range(8)]
            for v in halves:
                if v == h:
                    cur = jnp.where(inside, 0.0, src) if invert else src
                else:
                    cur = w_ref[rng, LANES * v : LANES * v + LANES]
                a = low[0] * z[v][0]
                b = low[1] * z[v][1]
                for i in range(2, 8, 2):
                    a = a + low[i] * z[v][i]
                    b = b + low[i + 1] * z[v][i + 1]
                w_ref[rng, LANES * v : LANES * v + LANES] = cur - (a + b)


def factor_kernel(a_ref, r_ref, w_ref):
    w_ref[...] = jnp.zeros_like(w_ref)
    w_ref[:, 0:K] = a_ref[...]
    r_ref[...] = jnp.zeros_like(r_ref)

    def emit(p, v, out, lane, sub):
        if v is None:
            return
        value = jnp.where(lane + LANES * v >= sub + 8 * p, out, 0.0)
        if v == 0:
            r_ref[8 * p : 8 * p + 8, 0:LANES] = value
        else:
            r_ref[8 * p : 8 * p + 8, LANES:K] = value[:, 0 : K - LANES]

    eliminate(w_ref, emit, False)


def factor(local_gram):
    return pl.pallas_call(
        factor_kernel,
        out_shape=jax.ShapeDtypeStruct((K, K), F32),
        in_specs=[VMEM_SPEC],
        out_specs=VMEM_SPEC,
        scratch_shapes=[pltpu.VMEM((K, 2 * LANES), F32)],
        name="factor",
    )(local_gram)


def solve_kernel(scale, p_ref, r_ref, c_ref, growth_ref, w_ref, inv_ref):
    u0, u1, u2 = p_ref[0:64, :], p_ref[64:128, :], p_ref[128:192, :]
    t0, t1, t2 = jnp.transpose(u0), jnp.transpose(u1), jnp.transpose(u2)
    w_ref[0:64, 0:LANES] = u0
    w_ref[0:64, LANES:] = u1
    w_ref[64:128, 0:LANES] = jnp.concatenate([t0[64:128], u1[:, 64:128]], axis=1)
    w_ref[64:128, LANES:] = u2
    w_ref[128:192, 0:LANES] = jnp.concatenate([t1[0:64], t2[0:64]], axis=1)
    w_ref[128:192, LANES:] = pltpu.roll(u2, 64, 1)
    diagonal = [jnp.ones((8, LANES), F32), jnp.ones((8, LANES), F32)]

    def emit(p, v, out, lane, sub):
        if v is None:
            h, l0 = 8 * p // LANES, 8 * p % LANES
            for i in range(8):
                diagonal[h] = jnp.where(lane == l0 + i, out[i], diagonal[h])
            return
        value = jnp.where(lane + LANES * v <= sub + 8 * p, out, 0.0)
        inv_ref[8 * p : 8 * p + 8, LANES * v : LANES * v + LANES] = value

    eliminate(w_ref, emit, True)
    growth_ref[0:1, 0:LANES] = 0.5 * jnp.log(diagonal[0][0:1, :])
    growth_ref[0:1, LANES:K] = 0.5 * jnp.log(diagonal[1][0:1, 0 : K - LANES])
    c_ref[...] = scale * lax.dot_general(
        r_ref[...], inv_ref[:, 0:K], (((1,), (1,)), ((), ())),
        precision=lax.Precision.HIGHEST, preferred_element_type=F32,
    )


def solve(scale, packed, local_factor):
    return pl.pallas_call(
        functools.partial(solve_kernel, scale),
        out_shape=(jax.ShapeDtypeStruct((K, K), F32), jax.ShapeDtypeStruct((1, K), F32)),
        in_specs=[VMEM_SPEC] * 2,
        out_specs=[VMEM_SPEC] * 2,
        scratch_shapes=[pltpu.VMEM((K, 2 * LANES), F32)] * 2,
        name="solve",
    )(packed, local_factor)


def per_device(groups, tiles, tangents, reaction_self, reaction_cross):
    packed, left, right = pack(tangents, reaction_self, reaction_cross)
    evolved = stencil(groups, tiles, packed, left, right)
    local_gram, local_packed = gram(evolved)
    local_factor = factor(local_gram)
    total = reduce_all(groups, tiles, local_packed)
    corrections, growth = solve(math.sqrt(groups * tiles), total, local_factor)
    return (corrections, growth.reshape(K))


def solution(mesh):
    groups, tiles = mesh.shape["grp"], mesh.shape["tile"]
    in_specs = (P(None, None, "tile", "grp"), P("tile", "grp"), P("tile", "grp"))
    out_specs = (P(("grp", "tile"), None), P())
    return jax.shard_map(
        functools.partial(per_device, groups, tiles),
        mesh=mesh, in_specs=in_specs, out_specs=out_specs, check_vma=False,
    )
```

```python
import functools
import math

import jax
import jax.numpy as jnp
from jax import lax
from jax.experimental import pallas as pl
from jax.experimental.pallas import tpu as pltpu
from jax.sharding import PartitionSpec as P

MESH = pl.DeviceIdType.MESH
F32 = jnp.float32
STEPS = 4
K = 192
NYD = 8
LANES = 128
ROWS = K + 8
BLOCKS_K = ROWS // 8
CHUNKS = 5
CHUNK = ROWS // CHUNKS
PER_CHUNK = CHUNK // 8
EDGE = STEPS
EXT = NYD + 2 * EDGE
DIFFUSION = 0.2
SLOW_RATE = 0.05
LIMIT = 12 << 20
VMEM_SPEC = pl.BlockSpec(memory_space=pltpu.VMEM)
NEIGHBOURS = [(dg, dt) for dg in (-1, 0, 1) for dt in (-1, 0, 1) if (dg, dt) != (0, 0)]


def lanes_of(shape=(8, LANES)):
    return lax.broadcasted_iota(jnp.int32, shape, 1)


def pack_kernel(tan_ref, self_ref, cross_ref, t_ref, left_ref, right_ref):
    lane = lanes_of()
    sub = lax.broadcasted_iota(jnp.int32, (8, LANES), 0)

    def body(fy, _):
        f = fy // NYD
        y = fy - f * NYD
        base = f * (K * NYD) + y
        own_self = jnp.broadcast_to(self_ref[pl.ds(y, 1), :], (8, LANES))
        own_cross = jnp.broadcast_to(cross_ref[pl.ds(y, 1), :], (8, LANES))
        block = jnp.where(sub == 0, own_self, own_cross)
        left = jnp.zeros((8, LANES), F32)
        right = jnp.zeros((8, LANES), F32)
        for b in range(BLOCKS_K):
            if b > 0:
                block = tan_ref[pl.ds(base + 64 * (b - 1), 8, stride=NYD), :]
            t_ref[fy, 8 * b : 8 * b + 8, :] = block
            here = (lane >= EDGE * b) & (lane < EDGE * b + EDGE)
            left = jnp.where(here, pltpu.roll(block, EDGE * b, 1) if b else block, left)
            right = jnp.where(here, pltpu.roll(block, (EDGE * b + EDGE) % LANES, 1), right)
        left_ref[fy] = left
        right_ref[fy] = right
        return 0

    lax.fori_loop(0, 2 * NYD, body, 0)


def pack(tangents, reaction_self, reaction_cross):
    return pl.pallas_call(
        pack_kernel,
        out_shape=(
            jax.ShapeDtypeStruct((2 * NYD, ROWS, LANES), F32),
            jax.ShapeDtypeStruct((2 * NYD, 8, LANES), F32),
            jax.ShapeDtypeStruct((2 * NYD, 8, LANES), F32),
        ),
        in_specs=[VMEM_SPEC] * 3,
        out_specs=[VMEM_SPEC] * 3,
        compiler_params=pltpu.CompilerParams(vmem_limit_bytes=LIMIT),
        name="pack",
    )(tangents.reshape(2 * K * NYD, LANES), reaction_self, reaction_cross)


def stencil_kernel(
    groups, tiles,
    t_ref, left_ref, right_ref, e_ref,
    up_ref, down_ref, xl_ref, xr_ref, co_ref,
    row_send, row_recv, edge_send, edge_recv,
):
    g = lax.axis_index("grp")
    t = lax.axis_index("tile")
    has = {-1: t > 0, 0: None, 1: t < tiles - 1}
    hasg = {-1: g > 0, 0: None, 1: g < groups - 1}

    def exists(dg, dt):
        terms = [c for c in (hasg[dg], has[dt]) if c is not None]
        return terms[0] if len(terms) == 1 else terms[0] & terms[1]

    barrier = pltpu.get_barrier_semaphore()
    for dg, dt in NEIGHBOURS:
        @pl.when(exists(dg, dt))
        def _():
            pl.semaphore_signal(barrier, inc=1, device_id=(g + dg, t + dt), device_id_type=MESH)
    wide_g = 1 + (g > 0).astype(jnp.int32) + (g < groups - 1).astype(jnp.int32)
    wide_t = 1 + (t > 0).astype(jnp.int32) + (t < tiles - 1).astype(jnp.int32)
    pl.semaphore_wait(barrier, wide_g * wide_t - 1)

    def row_copies(direction, c):
        rows = pl.ds(pl.multiple_of(c * CHUNK, 8), CHUNK)
        if direction == 0:
            fast, slow, dst, dt = slice(0, 4), slice(8, 11), down_ref, -1
        else:
            fast, slow, dst, dt = slice(4, 8), slice(13, 16), up_ref, 1
        out = []
        for i, (src, where) in enumerate(((fast, slice(0, 4)), (slow, slice(4, 7)))):
            out.append(
                pltpu.make_async_remote_copy(
                    src_ref=t_ref.at[src, rows, :],
                    dst_ref=dst.at[where, rows, :],
                    send_sem=row_send.at[direction, c, i],
                    recv_sem=row_recv.at[direction, c, i],
                    device_id=(g, t + dt),
                    device_id_type=MESH,
                )
            )
        return out

    def edge_copies(side, dt):
        src = left_ref if side == 0 else right_ref
        dst = xr_ref if side == 0 else xl_ref
        dg = -1 if side == 0 else 1
        rows, where = {
            -1: (slice(0, 4), slice(12, 16)),
            0: (slice(0, 8), slice(4, 12)),
            1: (slice(4, 8), slice(0, 4)),
        }[dt]
        out = []
        for f in range(2):
            out.append(
                pltpu.make_async_remote_copy(
                    src_ref=src.at[slice(8 * f + rows.start, 8 * f + rows.stop)],
                    dst_ref=dst.at[slice(EXT * f + where.start, EXT * f + where.stop)],
                    send_sem=edge_send.at[side, dt + 1, f],
                    recv_sem=edge_recv.at[side, dt + 1, f],
                    device_id=(g + dg, t + dt),
                    device_id_type=MESH,
                )
            )
        return dg, out

    for direction, dt in ((0, -1), (1, 1)):
        @pl.when(has[dt])
        def _():
            for copy in row_copies(direction, 0):
                copy.start()
    for side in range(2):
        for dt in (0, -1, 1):
            dg, copies = edge_copies(side, dt)

            @pl.when(exists(dg, dt))
            def _():
                for copy in copies:
                    copy.start()
    for direction, dt in ((0, -1), (1, 1)):
        @pl.when(has[dt])
        def _():
            def start(c, _):
                for copy in row_copies(direction, c):
                    copy.start()
                return 0

            lax.fori_loop(1, CHUNKS, start, 0)

    def wait_rows(c):
        for direction, dt in ((0, 1), (1, -1)):
            @pl.when(has[dt])
            def _():
                for copy in row_copies(direction, c):
                    copy.wait_recv()

    for side in range(2):
        for dt in (0, -1, 1):
            dg, copies = edge_copies(side, dt)

            @pl.when(exists(-dg, -dt))
            def _():
                for copy in copies:
                    copy.wait_recv()

    wait_rows(0)

    lane = lanes_of()
    zero = jnp.zeros((8, LANES), jnp.int32)
    first_lane = lane == 0
    last_lane = lane == LANES - 1
    wall_left = first_lane & (zero + g == 0)
    wall_right = last_lane & (zero + g == groups - 1)
    wall_top = zero + t == 0
    wall_bottom = zero + t == tiles - 1
    near = lane < EDGE
    far = lane >= LANES - EDGE

    def main_of(f, e, b):
        rows = pl.ds(pl.multiple_of(8 * b, 8), 8)
        if e < EDGE:
            return up_ref[e if f == 0 else 4 + e - 1, rows, :]
        if e < EDGE + NYD:
            return t_ref[NYD * f + e - EDGE, rows, :]
        return down_ref[e - 12 + 4 * f, rows, :]

    def halo_of(f, e, b):
        to_low = lax.rem(LANES - EDGE * b, LANES)
        to_high = LANES - EDGE - EDGE * b
        from_right = pltpu.roll(xr_ref[EXT * f + e], to_low, 1)
        from_left = pltpu.roll(xl_ref[EXT * f + e], to_high, 1)
        return jnp.where(near, from_right, jnp.where(far, from_left, 0.0))

    for e in range(1, EXT - 1):
        for part, block in enumerate((main_of(0, e, 0), halo_of(0, e, jnp.int32(0)))):
            own = jnp.broadcast_to(block[0:1, :], (8, LANES)) + (1.0 - 4.0 * DIFFUSION)
            co_ref[part, 0, e] = own
            co_ref[part, 1, e] = jnp.broadcast_to(block[1:2, :], (8, LANES))

    def sides(value):
        main, halo = value
        lm, lh = pltpu.roll(main, 1, 1), pltpu.roll(halo, 1, 1)
        rm, rh = pltpu.roll(main, LANES - 1, 1), pltpu.roll(halo, LANES - 1, 1)
        left = jnp.where(wall_left, main, jnp.where(first_lane, lh, lm))
        right = jnp.where(wall_right, main, jnp.where(last_lane, rh, rm))
        return (
            left + right,
            jnp.where(first_lane, lm, lh) + jnp.where(last_lane, rm, rh),
        )

    def compute(b):
        fast = [[None] * EXT for _ in range(STEPS + 1)]
        slow = [[None] * EXT for _ in range(STEPS + 1)]
        for e in range(EXT):
            fast[0][e] = (main_of(0, e, b), halo_of(0, e, b))
            if 1 <= e < EXT - 1:
                slow[0][e] = (main_of(1, e, b), halo_of(1, e, b))
            for s in range(1, STEPS + 1):
                r = e - s
                if r < s or r > EXT - 1 - s:
                    continue
                old, old_slow = fast[s - 1][r], slow[s - 1][r]
                north, south = fast[s - 1][r - 1], fast[s - 1][r + 1]
                side = sides(old)
                new, new_slow = [], []
                for part in range(2 if s < STEPS else 1):
                    up, down = north[part], south[part]
                    if r == EDGE:
                        up = jnp.where(wall_top, old[part], up)
                    if r == EDGE + NYD - 1:
                        down = jnp.where(wall_bottom, old[part], down)
                    total = (up + down) + side[part]
                    new.append(
                        co_ref[part, 0, r] * old[part]
                        + DIFFUSION * total
                        + co_ref[part, 1, r] * old_slow[part]
                    )
                    new_slow.append(old_slow[part] + SLOW_RATE * (old[part] - old_slow[part]))
                fast[s][r] = tuple(new)
                slow[s][r] = tuple(new_slow)
                if s == STEPS:
                    rows = pl.ds(pl.multiple_of(8 * (b - 1), 8), 8)
                    e_ref[r - EDGE, rows, :] = new[0]
                    e_ref[NYD + r - EDGE, rows, :] = new_slow[0]

    def chunk(first, count):
        def body(i, _):
            compute(first + i)
            return 0

        lax.fori_loop(0, count, body, 0)

    chunk(1, PER_CHUNK - 1)

    def rest(c, _):
        wait_rows(c)
        chunk(c * PER_CHUNK, PER_CHUNK)
        return 0

    lax.fori_loop(1, CHUNKS, rest, 0)

    for direction, dt in ((0, -1), (1, 1)):
        @pl.when(has[dt])
        def _():
            def finish(c, _):
                for copy in row_copies(direction, c):
                    copy.wait_send()
                return 0

            lax.fori_loop(0, CHUNKS, finish, 0)
    for side in range(2):
        for dt in (0, -1, 1):
            dg, copies = edge_copies(side, dt)

            @pl.when(exists(dg, dt))
            def _():
                for copy in copies:
                    copy.wait_send()


def stencil(groups, tiles, packed, left, right):
    return pl.pallas_call(
        functools.partial(stencil_kernel, groups, tiles),
        out_shape=jax.ShapeDtypeStruct((2 * NYD, K, LANES), F32),
        in_specs=[VMEM_SPEC] * 3,
        out_specs=VMEM_SPEC,
        scratch_shapes=[
            pltpu.VMEM((7, ROWS, LANES), F32),
            pltpu.VMEM((7, ROWS, LANES), F32),
            pltpu.VMEM((2 * EXT, 8, LANES), F32),
            pltpu.VMEM((2 * EXT, 8, LANES), F32),
            pltpu.VMEM((2, 2, EXT, 8, LANES), F32),
            pltpu.SemaphoreType.DMA((2, CHUNKS, 2)),
            pltpu.SemaphoreType.DMA((2, CHUNKS, 2)),
            pltpu.SemaphoreType.DMA((2, 3, 2)),
            pltpu.SemaphoreType.DMA((2, 3, 2)),
        ],
        compiler_params=pltpu.CompilerParams(collective_id=0, has_side_effects=True, vmem_limit_bytes=LIMIT),
        name="stencil",
    )(packed, left, right)


def eliminate(w_ref, emit, invert):
    lane = lanes_of()
    sub = lax.broadcasted_iota(jnp.int32, (8, LANES), 0)
    panels = K // 8
    for p in range(panels):
        j0 = 8 * p
        h, l0 = j0 // LANES, j0 % LANES
        halves = (0, 1) if invert else tuple(range(h, 2))
        inside = (lane >= l0) & (lane < l0 + 8)
        blk = {v: w_ref[j0 : j0 + 8, LANES * v : LANES * v + LANES] for v in halves}
        cols = [jnp.broadcast_to(blk[h][:, l0 + i : l0 + i + 1], (8, LANES)) for i in range(8)]
        el = [
            [jnp.broadcast_to(cols[i][m : m + 1, :], (8, LANES)) if m >= i else None for i in range(8)]
            for m in range(8)
        ]
        if invert:
            blk[h] = jnp.where(inside, jnp.where(lane - l0 == sub, 1.0, 0.0), blk[h])
        rows = {v: [jnp.broadcast_to(blk[v][m : m + 1, :], (8, LANES)) for m in range(8)] for v in halves}
        fac = [[None] * 8 for _ in range(8)]
        r, r2, pivots = [], [], []
        for i in range(8):
            pivots.append(el[i][i])
            r.append(lax.rsqrt(el[i][i]))
            r2.append(r[i] * r[i])
            for m in range(i + 1, 8):
                fac[m][i] = el[m][i] * r2[i]
            for k in range(i + 1, 8):
                for m in range(k, 8):
                    el[m][k] = el[m][k] - fac[k][i] * el[m][i]
            for v in halves:
                for m in range(i + 1, 8):
                    rows[v][m] = rows[v][m] - fac[m][i] * rows[v][i]
        for v in halves:
            out = rows[v][0] * r[0]
            for i in range(1, 8):
                out = jnp.where(sub == i, rows[v][i] * r[i], out)
            emit(p, v, out, lane, sub)
        emit(p, None, pivots, lane, sub)
        if p == panels - 1:
            break
        z = {v: [None] * 8 for v in halves}
        for v in halves:
            for i in range(7, -1, -1):
                acc = rows[v][i] * r2[i]
                for m in range(7, i, -1):
                    acc = acc - fac[m][i] * z[v][m]
                z[v][i] = acc
        for s in range(p + 1, panels):
            rng = slice(8 * s, 8 * s + 8)
            src = w_ref[rng, LANES * h : LANES * h + LANES]
            low = [jnp.broadcast_to(src[:, l0 + i : l0 + i + 1], (8, LANES)) for i in range(8)]
            for v in halves:
                if v == h:
                    cur = jnp.where(inside, 0.0, src) if invert else src
                else:
                    cur = w_ref[rng, LANES * v : LANES * v + LANES]
                a = low[0] * z[v][0]
                b = low[1] * z[v][1]
                for i in range(2, 8, 2):
                    a = a + low[i] * z[v][i]
                    b = b + low[i + 1] * z[v][i + 1]
                w_ref[rng, LANES * v : LANES * v + LANES] = cur - (a + b)
        yield


def split(a):
    high = a.astype(jnp.bfloat16)
    rest = a - high.astype(F32)
    middle = rest.astype(jnp.bfloat16)
    return high, middle, (rest - middle.astype(F32)).astype(jnp.bfloat16)


def gram_of(e_ref):
    def product(a, b):
        return lax.dot_general(a, b, (((1,), (1,)), ((), ())), preferred_element_type=F32)

    same = jnp.zeros((K, K), F32)
    mixed = jnp.zeros((K, K), F32)
    for y in range(NYD):
        a = jnp.concatenate([e_ref[y], e_ref[NYD + y]], axis=1)
        high, middle, low = split(a)
        same = same + product(high, high) + product(middle, middle)
        mixed = mixed + product(high, middle) + product(high, low)
    return same + mixed + jnp.transpose(mixed)


def tail_kernel(
    groups, tiles,
    e_ref, o_ref, r_ref,
    p_ref, near_ref, y_ref, z_ref, w_ref, sends, recvs,
):
    g = lax.axis_index("grp")
    t = lax.axis_index("tile")
    inner = 8
    outer = tiles // inner
    piece = K // inner
    z = t // inner
    q = t - z * inner

    def in_line(d):
        return (g, z * inner + lax.rem(q + d, inner))

    def in_y(d):
        return (lax.rem(g + d, groups), t)

    def in_z(d):
        return (g, lax.rem(z + d, outer) * inner + q)

    peers = (
        [in_line(d) for d in range(1, inner)]
        + [in_y(d) for d in range(1, groups)]
        + [in_z(d) for d in range(1, outer)]
    )
    barrier = pltpu.get_barrier_semaphore()
    for peer in peers:
        pl.semaphore_signal(barrier, inc=1, device_id=peer, device_id_type=MESH)

    gram = gram_of(e_ref)
    w_ref[:, 0:LANES] = gram[:, 0:LANES]
    w_ref[:, LANES:K] = gram[:, LANES:K]
    w_ref[:, K : 2 * LANES] = jnp.zeros((K, 2 * LANES - K), F32)
    p_ref[0:64, :] = gram[0:64, 0:128]
    p_ref[64:128, :] = jnp.concatenate([gram[0:64, 128:192], gram[64:128, 64:128]], axis=1)
    p_ref[128:192, :] = jnp.concatenate([gram[64:128, 128:192], gram[128:192, 128:192]], axis=1)
    pl.semaphore_wait(barrier, len(peers))

    count = [0]

    def copy_to(src, dst, peer):
        i = count[0]
        count[0] += 1
        copy = pltpu.make_async_remote_copy(
            src_ref=src, dst_ref=dst, send_sem=sends.at[i], recv_sem=recvs.at[i],
            device_id=peer, device_id_type=MESH,
        )
        copy.start()
        return copy

    def rows(index):
        return pl.ds(pl.multiple_of(index * piece, 8), piece)

    def emit_factor(p, v, out, lane, sub):
        if v is None:
            return
        value = jnp.where(lane + LANES * v >= sub + 8 * p, out, 0.0)
        r_ref[8 * p : 8 * p + 8, LANES * v : LANES * v + LANES] = value

    r_ref[...] = jnp.zeros_like(r_ref)
    local = eliminate(w_ref, emit_factor, False)

    def advance(panels):
        for _ in range(panels):
            next(local, None)

    started = []
    phase = []
    for d in range(1, inner):
        phase.append(copy_to(p_ref.at[rows(lax.rem(q + d, inner))], near_ref.at[d - 1], in_line(d)))
    advance(6)
    total = p_ref[rows(q), :]
    for d, copy in enumerate(phase):
        copy.wait_recv()
        total = total + near_ref[d]
    started += phase
    for buf, me, size, peer_of in ((y_ref, g, groups, in_y), (z_ref, z, outer, in_z)):
        buf[me] = total
        phase = [copy_to(buf.at[me], buf.at[me], peer_of(d)) for d in range(1, size)]
        advance(5)
        for copy in phase:
            copy.wait_recv()
        total = buf[0]
        for i in range(1, size):
            total = total + buf[i]
        started += phase
    o_ref[rows(q), :] = total
    phase = [copy_to(o_ref.at[rows(q)], o_ref.at[rows(q)], in_line(d)) for d in range(1, inner)]
    advance(K // 8)
    for copy in phase:
        copy.wait_recv()
    started += phase
    for copy in started:
        copy.wait_send()


def solve_kernel(scale, o_ref, r_ref, c_ref, growth_ref, v_ref, inv_ref):
    u0, u1, u2 = o_ref[0:64, :], o_ref[64:128, :], o_ref[128:192, :]
    t0, t1, t2 = jnp.transpose(u0), jnp.transpose(u1), jnp.transpose(u2)
    v_ref[0:64, 0:LANES] = u0
    v_ref[0:64, LANES:] = u1
    v_ref[64:128, 0:LANES] = jnp.concatenate([t0[64:128], u1[:, 64:128]], axis=1)
    v_ref[64:128, LANES:] = u2
    v_ref[128:192, 0:LANES] = jnp.concatenate([t1[0:64], t2[0:64]], axis=1)
    v_ref[128:192, LANES:] = pltpu.roll(u2, 64, 1)
    diagonal = [jnp.ones((8, LANES), F32), jnp.ones((8, LANES), F32)]

    def emit_inverse(p, v, out, lane, sub):
        if v is None:
            h, l0 = 8 * p // LANES, 8 * p % LANES
            for i in range(8):
                diagonal[h] = jnp.where(lane == l0 + i, out[i], diagonal[h])
            return
        value = jnp.where(lane + LANES * v <= sub + 8 * p, out, 0.0)
        inv_ref[8 * p : 8 * p + 8, LANES * v : LANES * v + LANES] = value

    for _ in eliminate(v_ref, emit_inverse, True):
        pass
    growth_ref[0:1, 0:LANES] = 0.5 * jnp.log(diagonal[0][0:1, :])
    growth_ref[0:1, LANES:K] = 0.5 * jnp.log(diagonal[1][0:1, 0 : K - LANES])
    c_ref[...] = scale * lax.dot_general(
        r_ref[...], inv_ref[...], (((1,), (1,)), ((), ())),
        precision=lax.Precision.HIGHEST, preferred_element_type=F32,
    )


def tail(groups, tiles, evolved):
    copies = 2 * 7 + (groups - 1) + (tiles // 8 - 1)
    return pl.pallas_call(
        functools.partial(tail_kernel, groups, tiles),
        out_shape=(jax.ShapeDtypeStruct((K, LANES), F32), jax.ShapeDtypeStruct((K, 2 * LANES), F32)),
        in_specs=[VMEM_SPEC],
        out_specs=[VMEM_SPEC] * 2,
        scratch_shapes=[
            pltpu.VMEM((K, LANES), F32),
            pltpu.VMEM((7, K // 8, LANES), F32),
            pltpu.VMEM((groups, K // 8, LANES), F32),
            pltpu.VMEM((tiles // 8, K // 8, LANES), F32),
            pltpu.VMEM((K, 2 * LANES), F32),
            pltpu.SemaphoreType.DMA((copies,)),
            pltpu.SemaphoreType.DMA((copies,)),
        ],
        compiler_params=pltpu.CompilerParams(collective_id=1, has_side_effects=True, vmem_limit_bytes=LIMIT),
        name="tail",
    )(evolved)


def solve(scale, reduced, local_factor):
    return pl.pallas_call(
        functools.partial(solve_kernel, scale),
        out_shape=(jax.ShapeDtypeStruct((K, K), F32), jax.ShapeDtypeStruct((1, K), F32)),
        in_specs=[VMEM_SPEC] * 2,
        out_specs=[VMEM_SPEC] * 2,
        scratch_shapes=[pltpu.VMEM((K, 2 * LANES), F32)] * 2,
        compiler_params=pltpu.CompilerParams(vmem_limit_bytes=LIMIT),
        name="solve",
    )(reduced, local_factor)


def per_device(groups, tiles, tangents, reaction_self, reaction_cross):
    packed, left, right = pack(tangents, reaction_self, reaction_cross)
    evolved = stencil(groups, tiles, packed, left, right)
    reduced, local_factor = tail(groups, tiles, evolved)
    corrections, growth = solve(math.sqrt(groups * tiles), reduced, local_factor)
    return (corrections, growth.reshape(K))


def solution(mesh):
    groups, tiles = mesh.shape["grp"], mesh.shape["tile"]
    in_specs = (P(None, None, "tile", "grp"), P("tile", "grp"), P("tile", "grp"))
    out_specs = (P(("grp", "tile"), None), P())
    return jax.shard_map(
        functools.partial(per_device, groups, tiles),
        mesh=mesh, in_specs=in_specs, out_specs=out_specs, check_vma=False,
    )
```

```python
import functools
import math

import jax
import jax.numpy as jnp
from jax import lax
from jax.experimental import pallas as pl
from jax.experimental.pallas import tpu as pltpu
from jax.sharding import PartitionSpec as P

MESH = pl.DeviceIdType.MESH
F32 = jnp.float32
STEPS = 4
K = 192
NYD = 8
LANES = 128
BLOCKS_K = K // 8
GROUPS_K = BLOCKS_K // 8
PER_CHUNK = 4
CHUNKS = BLOCKS_K // PER_CHUNK
CHUNK = 8 * PER_CHUNK
WINDOW = 3
TOGETHER = 2
COEF = GROUPS_K
SLOTS = 2 * GROUPS_K + 1
PAIRS = ((0, 1), (2, 6), (4, 5), (COEF, None))
EDGE = STEPS
EXT = NYD + 2 * EDGE
DIFFUSION = 0.2
SLOW_RATE = 0.05
LIMIT = 12 << 20
VMEM_SPEC = pl.BlockSpec(memory_space=pltpu.VMEM)
NEIGHBOURS = [(dg, dt) for dg in (-1, 0, 1) for dt in (-1, 0, 1) if (dg, dt) != (0, 0)]


def lanes_of(shape=(8, LANES)):
    return lax.broadcasted_iota(jnp.int32, shape, 1)


def front_kernel(
    groups, tiles,
    tan_hbm, self_hbm, cross_hbm, e_ref,
    cells_ref, cf_ref, o_ref, t_ref, x_ref, q_ref, out_ref, co_ref,
    local_sem, cf_sem, cf_send, cf_recv, row_send, row_recv, edge_send, edge_recv,
):
    g = lax.axis_index("grp")
    t = lax.axis_index("tile")
    has = {-1: t > 0, 0: None, 1: t < tiles - 1}
    hasg = {-1: g > 0, 0: None, 1: g < groups - 1}

    def exists(dg, dt):
        terms = [c for c in (hasg[dg], has[dt]) if c is not None]
        return terms[0] if len(terms) == 1 else terms[0] & terms[1]

    barrier = pltpu.get_barrier_semaphore()
    for dg, dt in NEIGHBOURS:
        @pl.when(exists(dg, dt))
        def _():
            pl.semaphore_signal(barrier, inc=1, device_id=(g + dg, t + dt), device_id_type=MESH)

    def fields_of(c):
        return pl.ds(c * CHUNK if isinstance(c, int) else pl.multiple_of(c * CHUNK, 8), CHUNK)

    def local_copy(group):
        fields = pl.ds(64 * group, 64)
        return pltpu.make_async_copy(tan_hbm.at[:, fields], cells_ref.at[0, :, fields], local_sem.at[group])

    cf_copies = [
        pltpu.make_async_copy(src, cf_ref.at[0, i], cf_sem.at[i]) for i, src in enumerate((self_hbm, cross_hbm))
    ]
    for copy in cf_copies:
        copy.start()
    for group in range(GROUPS_K):
        local_copy(group).start()

    def row_copies(direction, c):
        fields = fields_of(c)
        spans = (slice(0, 4), slice(0, 3)) if direction == 0 else (slice(4, 8), slice(5, 8))
        return [
            pltpu.make_async_remote_copy(
                src_ref=cells_ref.at[0, f, fields, spans[f], :],
                dst_ref=cells_ref.at[1, f, fields, spans[f], :],
                send_sem=row_send.at[direction, c, f],
                recv_sem=row_recv.at[direction, c, f],
                device_id=(g, t + (1 if direction else -1)),
                device_id_type=MESH,
            )
            for f in range(2)
        ]

    def cf_copy(direction):
        return pltpu.make_async_remote_copy(
            src_ref=cf_ref.at[0],
            dst_ref=cf_ref.at[1 + direction],
            send_sem=cf_send.at[direction],
            recv_sem=cf_recv.at[direction],
            device_id=(g, t + (1 if direction else -1)),
            device_id_type=MESH,
        )

    def edge_copy(side, dt):
        rows = {-1: slice(0, 4), 0: slice(0, 8), 1: slice(4, 8)}[dt]
        return pltpu.make_async_remote_copy(
            src_ref=t_ref.at[rows],
            dst_ref=x_ref.at[side, 1 - dt, rows],
            send_sem=edge_send.at[side, 1 - dt],
            recv_sem=edge_recv.at[side, 1 - dt],
            device_id=(g + (1 if side else -1), t + dt),
            device_id_type=MESH,
        )

    lane = lanes_of()
    sub = lax.broadcasted_iota(jnp.int32, (8, LANES), 0)
    within = lane & 15
    shared = ((lane + EDGE) & 15) < 2 * EDGE
    cell_rows = cells_ref.reshape(2 * 2 * K * NYD, LANES)
    halo = 2 * K * NYD
    top, bottom = t == 0, t == tiles - 1

    def row_of(e):
        above = e < EDGE
        below = e >= EDGE + NYD
        where = jnp.where(above & ~top, 0, jnp.where(below & ~bottom, 2, 1))
        y = jnp.where(
            above,
            jnp.where(top, EDGE - 1 - e, e + NYD - EDGE),
            jnp.where(below & bottom, EDGE + 2 * NYD - 1 - e, e - EDGE - jnp.where(below, NYD, 0)),
        )
        return where, y

    row_at = [
        (1, e - EDGE) if EDGE <= e < EDGE + NYD else row_of(jnp.int32(e)) for e in range(EXT)
    ]

    def main_of(f, e, b):
        base = f * (K * NYD) + 64 * b
        where, y = row_at[e]
        if e < EDGE or e >= EDGE + NYD:
            base = base + jnp.where(where == 1, 0, halo)
        return cell_rows[pl.ds(base + y, 8, stride=NYD), :]

    def pack_coefs(e):
        where, y = row_at[e]
        source = 0 if isinstance(where, int) else jnp.where(where == 1, 0, 2 if e < EDGE else 1)
        rows = [jnp.broadcast_to(cf_ref[source, i, pl.ds(y, 1), :], (8, LANES)) for i in range(2)]
        block = jnp.where(sub == 0, rows[0], rows[1])
        block = jnp.where((lane < 8) | (lane >= LANES - 8), block, 0.0)
        for shift in (16, 32, 64):
            block = block + pltpu.roll(block, shift, 1)
        o_ref[e, COEF] = block
        own = rows[0]
        co_ref[0, 0, e] = (own + (1.0 - 4.0 * DIFFUSION)) * (1.0 / DIFFUSION)
        for s in range(1, STEPS + 1):
            co_ref[0, s, e] = rows[1] * ((1.0 - SLOW_RATE) ** (s - 1) / DIFFUSION**s)

    for copy in cf_copies:
        copy.wait()
    for y in range(NYD):
        pack_coefs(EDGE + y)
    for group in range(GROUPS_K):
        local_copy(group).wait()

        def pack_row(y, _):
            for f in range(2):
                packed = None
                for m in range(8):
                    block = cell_rows[pl.ds(f * (K * NYD) + 64 * (8 * group + m) + y, 8, stride=NYD), :]
                    if m == 0:
                        packed = block
                    else:
                        packed = jnp.where(
                            (lane >= 16 * m - 8) & (lane < 16 * m + 8), pltpu.roll(block, 16 * m, 1), packed
                        )
                o_ref[EDGE + y, f * (GROUPS_K + 1) + group] = packed
            return 0

        lax.fori_loop(0, NYD, pack_row, 0)

    def share_row(y, _):
        for i, (one, two) in enumerate(PAIRS):
            value = o_ref[EDGE + y, one]
            if two is not None:
                value = jnp.where(shared, value, pltpu.roll(o_ref[EDGE + y, two], 8, 1))
            t_ref[y, i] = value
        return 0

    lax.fori_loop(0, NYD, share_row, 0)

    wide_g = 1 + (g > 0).astype(jnp.int32) + (g < groups - 1).astype(jnp.int32)
    wide_t = 1 + (t > 0).astype(jnp.int32) + (t < tiles - 1).astype(jnp.int32)
    pl.semaphore_wait(barrier, wide_g * wide_t - 1)

    def send(c):
        for direction in range(2):
            @pl.when(has[1 if direction else -1])
            def _():
                for copy in row_copies(direction, c):
                    copy.start()

    def receive(c):
        for direction in range(2):
            @pl.when(has[-1 if direction else 1])
            def _():
                for copy in row_copies(direction, c):
                    copy.wait_recv()

    def settle(c):
        for direction in range(2):
            @pl.when(has[1 if direction else -1])
            def _():
                for copy in row_copies(direction, c):
                    copy.wait_send()

    for direction in range(2):
        @pl.when(has[1 if direction else -1])
        def _():
            cf_copy(direction).start()
    send(0)
    for dt in (0, -1, 1):
        for side in range(2):
            @pl.when(exists(1 if side else -1, dt))
            def _():
                edge_copy(side, dt).start()
    for c in range(1, WINDOW):
        send(c)
    for direction in range(2):
        @pl.when(has[-1 if direction else 1])
        def _():
            cf_copy(direction).wait_recv()
    for e in range(EXT):
        if e < EDGE or e >= EDGE + NYD:
            pack_coefs(e)

    def evolve(loads, coefs, stores):
        lots = range(len(loads))
        fast = [[[None] * EXT for _ in range(STEPS + 1)] for _ in lots]
        slow = [[[None] * EXT for _ in range(STEPS + 1)] for _ in lots]
        for e in range(EXT):
            for n in lots:
                fast[n][0][e] = loads[n](0, e)
                if 1 <= e < EXT - 1:
                    slow[n][0][e] = loads[n](1, e)
            for s in range(1, STEPS + 1):
                r = e - s
                if r < s or r > EXT - 1 - s:
                    continue
                drift = SLOW_RATE * DIFFUSION ** (s - 1) / (1.0 - SLOW_RATE) ** s
                for n in lots:
                    before = fast[n][s - 1]
                    old, old_slow = before[r], slow[n][s - 1][r]
                    total = (before[r - 1] + before[r + 1]) + (
                        pltpu.roll(old, 1, 1) + pltpu.roll(old, LANES - 1, 1)
                    )
                    new = total + (coefs[n](0, r) * old + coefs[n](s, r) * old_slow)
                    new_slow = old_slow + drift * old
                    fast[n][s][r] = new
                    slow[n][s][r] = new_slow
                    if s == STEPS:
                        stores[n](r - EDGE, new * DIFFUSION**STEPS)
                        stores[n](NYD + r - EDGE, new_slow * (1.0 - SLOW_RATE) ** STEPS)

    def block_steps(first):
        loads, stores = [], []
        for n in range(TOGETHER):
            b = first + n
            group = b // 8
            m = b - 8 * group
            rows = pl.ds(pl.multiple_of(8 * b, 8), 8)
            here = ((lane + 8) & (LANES - 1)) // 16 == m

            def load(f, e, b=b, group=group, m=m, here=here):
                value = main_of(f, e, b)
                if e < EDGE or e >= EDGE + NYD:
                    slot = f * (GROUPS_K + 1) + group
                    o_ref[e, slot] = jnp.where(here, pltpu.roll(value, 16 * m, 1), o_ref[e, slot])
                return value

            def store(fy, value, rows=rows):
                e_ref[fy, rows, :] = value

            loads.append(load)
            stores.append(store)
        evolve(loads, [lambda s, r: co_ref[0, s, r]] * TOGETHER, stores)

    def chunk(c, _):
        receive(c)

        @pl.when(c < CHUNKS - WINDOW)
        def _():
            send(c + WINDOW)

        def step(i, _):
            block_steps(PER_CHUNK * c + TOGETHER * i)
            return 0

        lax.fori_loop(0, PER_CHUNK // TOGETHER, step, 0)
        return 0

    lax.fori_loop(0, CHUNKS, chunk, 0)

    for dt in (0, -1, 1):
        for side in range(2):
            @pl.when(exists(-1 if side else 1, -dt))
            def _():
                edge_copy(side, dt).wait_recv()

    def join(side, e, slot, value):
        beside = within < EDGE if side == 0 else within >= 16 - EDGE
        q_ref[side, e, slot] = jnp.where(beside, value, o_ref[e, slot])

    for side in range(2):
        @pl.when(hasg[-1 if side else 1])
        def _():
            def join_row(k, _):
                for e in (4 * k, 4 * k + 1, 4 * k + 2, 4 * k + 3):
                    where, y = row_of(e)
                    for i, (one, two) in enumerate(PAIRS):
                        value = x_ref[side, where, y, i]
                        join(side, e, one, value)
                        if two is not None:
                            join(side, e, two, pltpu.roll(value, LANES - 8, 1))
                return 0

            lax.fori_loop(0, EXT // 4, join_row, 0)

        @pl.when(g == (0 if side else groups - 1))
        def _():
            def mirror_row(k, _):
                for e in (4 * k, 4 * k + 1, 4 * k + 2, 4 * k + 3):
                    for slot in range(SLOTS):
                        value = o_ref[e, slot]
                        flipped = None
                        for i in range(EDGE):
                            shift = LANES - 7 + 2 * i if side else 1 + 2 * i
                            moved = pltpu.roll(value, shift, 1)
                            flipped = moved if flipped is None else jnp.where((lane & 3) == i, moved, flipped)
                        join(side, e, slot, flipped)
                return 0

            lax.fori_loop(0, EXT // 4, mirror_row, 0)

    def side_coefs(k, _):
        for side, e in [(side, 2 * k - 1 + i) for side in range(2) for i in range(2)]:
            packed = q_ref[side, e, COEF]
            own = jnp.broadcast_to(packed[0:1, :], (8, LANES))
            cross = jnp.broadcast_to(packed[1:2, :], (8, LANES))
            co_ref[1 + side, 0, e] = (own + (1.0 - 4.0 * DIFFUSION)) * (1.0 / DIFFUSION)
            for s in range(1, STEPS + 1):
                co_ref[1 + side, s, e] = cross * ((1.0 - SLOW_RATE) ** (s - 1) / DIFFUSION**s)
        return 0

    lax.fori_loop(1, EXT // 2, side_coefs, 0)

    def side_step(group, _):
        loads, coefs, stores = [], [], []
        for side in range(2):
            loads.append(lambda f, e, side=side: q_ref[side, e, f * (GROUPS_K + 1) + group])
            coefs.append(lambda s, r, side=side: co_ref[1 + side, s, r])

            def store(fy, value, side=side):
                out_ref[side, fy, group] = value

            stores.append(store)
        evolve(loads, coefs, stores)
        return 0

    lax.fori_loop(0, GROUPS_K, side_step, 0)

    at_side = (lane < EDGE) | (lane >= LANES - EDGE)

    def merge(i, _):
        for fy in (4 * i, 4 * i + 1, 4 * i + 2, 4 * i + 3):
            for group in range(GROUPS_K):
                value = jnp.where(within < 8, out_ref[1, fy, group], out_ref[0, fy, group])
                for m in range(8):
                    rows = slice(64 * group + 8 * m, 64 * group + 8 * m + 8)
                    moved = pltpu.roll(value, LANES - 16 * m, 1) if m else value
                    e_ref[fy, rows, :] = jnp.where(at_side, moved, e_ref[fy, rows, :])
        return 0

    lax.fori_loop(0, NYD // 2, merge, 0)

    def finish(c, _):
        settle(c)
        return 0

    lax.fori_loop(0, CHUNKS, finish, 0)
    for dt in (0, -1, 1):
        for side in range(2):
            @pl.when(exists(1 if side else -1, dt))
            def _():
                edge_copy(side, dt).wait_send()
    for direction in range(2):
        @pl.when(has[1 if direction else -1])
        def _():
            cf_copy(direction).wait_send()


def front(groups, tiles, tangents, reaction_self, reaction_cross):
    hbm = pl.BlockSpec(memory_space=pltpu.HBM)
    return pl.pallas_call(
        functools.partial(front_kernel, groups, tiles),
        out_shape=jax.ShapeDtypeStruct((2 * NYD, K, LANES), F32),
        in_specs=[hbm] * 3,
        out_specs=VMEM_SPEC,
        scratch_shapes=[
            pltpu.VMEM((2, 2, K, NYD, LANES), F32),
            pltpu.VMEM((3, 2, NYD, LANES), F32),
            pltpu.VMEM((EXT, SLOTS, 8, LANES), F32),
            pltpu.VMEM((NYD, len(PAIRS), 8, LANES), F32),
            pltpu.VMEM((2, 3, NYD, len(PAIRS), 8, LANES), F32),
            pltpu.VMEM((2, EXT, SLOTS, 8, LANES), F32),
            pltpu.VMEM((2, 2 * NYD, GROUPS_K, 8, LANES), F32),
            pltpu.VMEM((3, STEPS + 1, EXT, 8, LANES), F32),
            pltpu.SemaphoreType.DMA((GROUPS_K,)),
            pltpu.SemaphoreType.DMA((2,)),
            pltpu.SemaphoreType.DMA((2,)),
            pltpu.SemaphoreType.DMA((2,)),
            pltpu.SemaphoreType.DMA((2, CHUNKS, 2)),
            pltpu.SemaphoreType.DMA((2, CHUNKS, 2)),
            pltpu.SemaphoreType.DMA((2, 3)),
            pltpu.SemaphoreType.DMA((2, 3)),
        ],
        compiler_params=pltpu.CompilerParams(
            collective_id=0, has_side_effects=True, vmem_limit_bytes=LIMIT
        ),
        name="front",
    )(*[pltpu.with_memory_space_constraint(x, pltpu.HBM) for x in (tangents, reaction_self, reaction_cross)])


def eliminate(w_ref, emit, invert):
    lane = lanes_of()
    sub = lax.broadcasted_iota(jnp.int32, (8, LANES), 0)
    panels = K // 8
    for p in range(panels):
        j0 = 8 * p
        h, l0 = j0 // LANES, j0 % LANES
        halves = (0, 1) if invert else tuple(range(h, 2))
        inside = (lane >= l0) & (lane < l0 + 8)
        blk = {v: w_ref[j0 : j0 + 8, LANES * v : LANES * v + LANES] for v in halves}
        cols = [jnp.broadcast_to(blk[h][:, l0 + i : l0 + i + 1], (8, LANES)) for i in range(8)]
        el = [
            [jnp.broadcast_to(cols[i][m : m + 1, :], (8, LANES)) if m >= i else None for i in range(8)]
            for m in range(8)
        ]
        if invert:
            blk[h] = jnp.where(inside, jnp.where(lane - l0 == sub, 1.0, 0.0), blk[h])
        rows = {v: [jnp.broadcast_to(blk[v][m : m + 1, :], (8, LANES)) for m in range(8)] for v in halves}
        fac = [[None] * 8 for _ in range(8)]
        r, r2, pivots = [], [], []
        for i in range(8):
            pivots.append(el[i][i])
            r.append(lax.rsqrt(el[i][i]))
            r2.append(r[i] * r[i])
            for m in range(i + 1, 8):
                fac[m][i] = el[m][i] * r2[i]
            for k in range(i + 1, 8):
                for m in range(k, 8):
                    el[m][k] = el[m][k] - fac[k][i] * el[m][i]
            for v in halves:
                for m in range(i + 1, 8):
                    rows[v][m] = rows[v][m] - fac[m][i] * rows[v][i]
        for v in halves:
            out = rows[v][0] * r[0]
            for i in range(1, 8):
                out = jnp.where(sub == i, rows[v][i] * r[i], out)
            emit(p, v, out, lane, sub)
        emit(p, None, pivots, lane, sub)
        if p == panels - 1:
            break
        z = {v: [None] * 8 for v in halves}
        for v in halves:
            for i in range(7, -1, -1):
                acc = rows[v][i] * r2[i]
                for m in range(7, i, -1):
                    acc = acc - fac[m][i] * z[v][m]
                z[v][i] = acc
        for s in range(p + 1, panels):
            rng = slice(8 * s, 8 * s + 8)
            src = w_ref[rng, LANES * h : LANES * h + LANES]
            low = [jnp.broadcast_to(src[:, l0 + i : l0 + i + 1], (8, LANES)) for i in range(8)]
            for v in halves:
                if v == h:
                    cur = jnp.where(inside, 0.0, src) if invert else src
                else:
                    cur = w_ref[rng, LANES * v : LANES * v + LANES]
                a = low[0] * z[v][0]
                b = low[1] * z[v][1]
                for i in range(2, 8, 2):
                    a = a + low[i] * z[v][i]
                    b = b + low[i + 1] * z[v][i + 1]
                w_ref[rng, LANES * v : LANES * v + LANES] = cur - (a + b)
        yield


def split(a):
    high = a.astype(jnp.bfloat16)
    rest = a - high.astype(F32)
    middle = rest.astype(jnp.bfloat16)
    return high, middle, (rest - middle.astype(F32)).astype(jnp.bfloat16)


def gram_of(e_ref):
    def product(a, b):
        return lax.dot_general(a, b, (((1,), (1,)), ((), ())), preferred_element_type=F32)

    same = jnp.zeros((K, K), F32)
    mixed = jnp.zeros((K, K), F32)
    for y in range(NYD):
        a = jnp.concatenate([e_ref[y], e_ref[NYD + y]], axis=1)
        high, middle, low = split(a)
        same = same + product(high, high) + product(middle, middle)
        mixed = mixed + product(high, middle) + product(high, low)
    return same + mixed + jnp.transpose(mixed)


def tail_kernel(
    groups, tiles,
    e_ref, o_ref, r_ref,
    p_ref, near_ref, y_ref, z_ref, w_ref, sends, recvs,
):
    g = lax.axis_index("grp")
    t = lax.axis_index("tile")
    inner = 8
    outer = tiles // inner
    piece = K // inner
    z = t // inner
    q = t - z * inner

    def in_line(d):
        return (g, z * inner + lax.rem(q + d, inner))

    def in_y(d):
        return (lax.rem(g + d, groups), t)

    def in_z(d):
        return (g, lax.rem(z + d, outer) * inner + q)

    peers = (
        [in_line(d) for d in range(1, inner)]
        + [in_y(d) for d in range(1, groups)]
        + [in_z(d) for d in range(1, outer)]
    )
    barrier = pltpu.get_barrier_semaphore()
    for peer in peers:
        pl.semaphore_signal(barrier, inc=1, device_id=peer, device_id_type=MESH)

    gram = gram_of(e_ref)
    w_ref[:, 0:LANES] = gram[:, 0:LANES]
    w_ref[:, LANES:K] = gram[:, LANES:K]
    w_ref[:, K : 2 * LANES] = jnp.zeros((K, 2 * LANES - K), F32)
    p_ref[0:64, :] = gram[0:64, 0:128]
    p_ref[64:128, :] = jnp.concatenate([gram[0:64, 128:192], gram[64:128, 64:128]], axis=1)
    p_ref[128:192, :] = jnp.concatenate([gram[64:128, 128:192], gram[128:192, 128:192]], axis=1)
    pl.semaphore_wait(barrier, len(peers))

    count = [0]

    def copy_to(src, dst, peer):
        i = count[0]
        count[0] += 1
        copy = pltpu.make_async_remote_copy(
            src_ref=src, dst_ref=dst, send_sem=sends.at[i], recv_sem=recvs.at[i],
            device_id=peer, device_id_type=MESH,
        )
        copy.start()
        return copy

    def rows(index):
        return pl.ds(pl.multiple_of(index * piece, 8), piece)

    def emit_factor(p, v, out, lane, sub):
        if v is None:
            return
        value = jnp.where(lane + LANES * v >= sub + 8 * p, out, 0.0)
        r_ref[8 * p : 8 * p + 8, LANES * v : LANES * v + LANES] = value

    r_ref[...] = jnp.zeros_like(r_ref)
    local = eliminate(w_ref, emit_factor, False)

    def advance(panels):
        for _ in range(panels):
            next(local, None)

    started = []
    phase = []
    for d in range(1, inner):
        phase.append(copy_to(p_ref.at[rows(lax.rem(q + d, inner))], near_ref.at[d - 1], in_line(d)))
    advance(6)
    total = p_ref[rows(q), :]
    for d, copy in enumerate(phase):
        copy.wait_recv()
        total = total + near_ref[d]
    started += phase
    for buf, me, size, peer_of in ((y_ref, g, groups, in_y), (z_ref, z, outer, in_z)):
        buf[me] = total
        phase = [copy_to(buf.at[me], buf.at[me], peer_of(d)) for d in range(1, size)]
        advance(5)
        for copy in phase:
            copy.wait_recv()
        total = buf[0]
        for i in range(1, size):
            total = total + buf[i]
        started += phase
    o_ref[rows(q), :] = total
    phase = [copy_to(o_ref.at[rows(q)], o_ref.at[rows(q)], in_line(d)) for d in range(1, inner)]
    advance(K // 8)
    for copy in phase:
        copy.wait_recv()
    started += phase
    for copy in started:
        copy.wait_send()


def solve_kernel(scale, o_ref, r_ref, c_ref, growth_ref, v_ref, inv_ref):
    u0, u1, u2 = o_ref[0:64, :], o_ref[64:128, :], o_ref[128:192, :]
    t0, t1, t2 = jnp.transpose(u0), jnp.transpose(u1), jnp.transpose(u2)
    v_ref[0:64, 0:LANES] = u0
    v_ref[0:64, LANES:] = u1
    v_ref[64:128, 0:LANES] = jnp.concatenate([t0[64:128], u1[:, 64:128]], axis=1)
    v_ref[64:128, LANES:] = u2
    v_ref[128:192, 0:LANES] = jnp.concatenate([t1[0:64], t2[0:64]], axis=1)
    v_ref[128:192, LANES:] = pltpu.roll(u2, 64, 1)
    diagonal = [jnp.ones((8, LANES), F32), jnp.ones((8, LANES), F32)]

    def emit_inverse(p, v, out, lane, sub):
        if v is None:
            h, l0 = 8 * p // LANES, 8 * p % LANES
            for i in range(8):
                diagonal[h] = jnp.where(lane == l0 + i, out[i], diagonal[h])
            return
        value = jnp.where(lane + LANES * v <= sub + 8 * p, out, 0.0)
        inv_ref[8 * p : 8 * p + 8, LANES * v : LANES * v + LANES] = value

    for _ in eliminate(v_ref, emit_inverse, True):
        pass
    growth_ref[0:1, 0:LANES] = 0.5 * jnp.log(diagonal[0][0:1, :])
    growth_ref[0:1, LANES:K] = 0.5 * jnp.log(diagonal[1][0:1, 0 : K - LANES])
    c_ref[...] = scale * lax.dot_general(
        r_ref[...], inv_ref[...], (((1,), (1,)), ((), ())),
        precision=lax.Precision.HIGHEST, preferred_element_type=F32,
    )


def tail(groups, tiles, evolved):
    copies = 2 * 7 + (groups - 1) + (tiles // 8 - 1)
    return pl.pallas_call(
        functools.partial(tail_kernel, groups, tiles),
        out_shape=(jax.ShapeDtypeStruct((K, LANES), F32), jax.ShapeDtypeStruct((K, 2 * LANES), F32)),
        in_specs=[VMEM_SPEC],
        out_specs=[VMEM_SPEC] * 2,
        scratch_shapes=[
            pltpu.VMEM((K, LANES), F32),
            pltpu.VMEM((7, K // 8, LANES), F32),
            pltpu.VMEM((groups, K // 8, LANES), F32),
            pltpu.VMEM((tiles // 8, K // 8, LANES), F32),
            pltpu.VMEM((K, 2 * LANES), F32),
            pltpu.SemaphoreType.DMA((copies,)),
            pltpu.SemaphoreType.DMA((copies,)),
        ],
        compiler_params=pltpu.CompilerParams(collective_id=1, has_side_effects=True, vmem_limit_bytes=LIMIT),
        name="tail",
    )(evolved)


def solve(scale, reduced, local_factor):
    return pl.pallas_call(
        functools.partial(solve_kernel, scale),
        out_shape=(jax.ShapeDtypeStruct((K, K), F32), jax.ShapeDtypeStruct((1, K), F32)),
        in_specs=[VMEM_SPEC] * 2,
        out_specs=[VMEM_SPEC] * 2,
        scratch_shapes=[pltpu.VMEM((K, 2 * LANES), F32)] * 2,
        compiler_params=pltpu.CompilerParams(vmem_limit_bytes=LIMIT),
        name="solve",
    )(reduced, local_factor)


def per_device(groups, tiles, tangents, reaction_self, reaction_cross):
    evolved = front(groups, tiles, tangents, reaction_self, reaction_cross)
    reduced, local_factor = tail(groups, tiles, evolved)
    corrections, growth = solve(math.sqrt(groups * tiles), reduced, local_factor)
    return (corrections, growth.reshape(K))


def solution(mesh):
    groups, tiles = mesh.shape["grp"], mesh.shape["tile"]
    in_specs = (P(None, None, "tile", "grp"), P("tile", "grp"), P("tile", "grp"))
    out_specs = (P(("grp", "tile"), None), P())
    return jax.shard_map(
        functools.partial(per_device, groups, tiles),
        mesh=mesh, in_specs=in_specs, out_specs=out_specs, check_vma=False,
    )
```

```python
import functools
import math

import jax
import jax.numpy as jnp
from jax import lax
from jax.experimental import pallas as pl
from jax.experimental.pallas import tpu as pltpu
from jax.sharding import PartitionSpec as P

MESH = pl.DeviceIdType.MESH
F32 = jnp.float32
STEPS = 4
K = 192
NYD = 8
LANES = 128
BLOCKS_K = K // 8
GROUPS_K = BLOCKS_K // 8
PER_CHUNK = 4
CHUNKS = BLOCKS_K // PER_CHUNK
CHUNK = 8 * PER_CHUNK
WINDOW = 3
TOGETHER = 2
COEF = GROUPS_K
SLOTS = 2 * GROUPS_K + 1
PAIRS = ((0, 1), (2, 6), (4, 5), (COEF, None))
EDGE = STEPS
EXT = NYD + 2 * EDGE
DIFFUSION = 0.2
SLOW_RATE = 0.05
LIMIT = 12 << 20
VMEM_SPEC = pl.BlockSpec(memory_space=pltpu.VMEM)
NEIGHBOURS = [(dg, dt) for dg in (-1, 0, 1) for dt in (-1, 0, 1) if (dg, dt) != (0, 0)]


def lanes_of(shape=(8, LANES)):
    return lax.broadcasted_iota(jnp.int32, shape, 1)


def front_part(
    groups, tiles, greeted,
    tan_hbm, self_hbm, cross_hbm, e_ref,
    cells_ref, cf_ref, o_ref, t_ref, x_ref, q_ref, out_ref, co_ref,
    local_sem, cf_sem, cf_send, cf_recv, row_send, row_recv, edge_send, edge_recv,
):
    g = lax.axis_index("grp")
    t = lax.axis_index("tile")
    has = {-1: t > 0, 0: None, 1: t < tiles - 1}
    hasg = {-1: g > 0, 0: None, 1: g < groups - 1}

    def exists(dg, dt):
        terms = [c for c in (hasg[dg], has[dt]) if c is not None]
        return terms[0] if len(terms) == 1 else terms[0] & terms[1]

    barrier = pltpu.get_barrier_semaphore()
    for dg, dt in NEIGHBOURS:
        @pl.when(exists(dg, dt))
        def _():
            pl.semaphore_signal(barrier, inc=1, device_id=(g + dg, t + dt), device_id_type=MESH)
    for peer in greeted:
        pl.semaphore_signal(barrier, inc=1, device_id=peer, device_id_type=MESH)

    def fields_of(c):
        return pl.ds(c * CHUNK if isinstance(c, int) else pl.multiple_of(c * CHUNK, 8), CHUNK)

    def local_copy(group):
        fields = pl.ds(64 * group, 64)
        return pltpu.make_async_copy(tan_hbm.at[:, fields], cells_ref.at[0, :, fields], local_sem.at[group])

    cf_copies = [
        pltpu.make_async_copy(src, cf_ref.at[0, i], cf_sem.at[i]) for i, src in enumerate((self_hbm, cross_hbm))
    ]
    for copy in cf_copies:
        copy.start()
    for group in range(GROUPS_K):
        local_copy(group).start()

    def row_copies(direction, c):
        fields = fields_of(c)
        spans = (slice(0, 4), slice(0, 3)) if direction == 0 else (slice(4, 8), slice(5, 8))
        return [
            pltpu.make_async_remote_copy(
                src_ref=cells_ref.at[0, f, fields, spans[f], :],
                dst_ref=cells_ref.at[1, f, fields, spans[f], :],
                send_sem=row_send.at[direction, c, f],
                recv_sem=row_recv.at[direction, c, f],
                device_id=(g, t + (1 if direction else -1)),
                device_id_type=MESH,
            )
            for f in range(2)
        ]

    def cf_copy(direction):
        return pltpu.make_async_remote_copy(
            src_ref=cf_ref.at[0],
            dst_ref=cf_ref.at[1 + direction],
            send_sem=cf_send.at[direction],
            recv_sem=cf_recv.at[direction],
            device_id=(g, t + (1 if direction else -1)),
            device_id_type=MESH,
        )

    def edge_copy(side, dt):
        rows = {-1: slice(0, 4), 0: slice(0, 8), 1: slice(4, 8)}[dt]
        return pltpu.make_async_remote_copy(
            src_ref=t_ref.at[rows],
            dst_ref=x_ref.at[side, 1 - dt, rows],
            send_sem=edge_send.at[side, 1 - dt],
            recv_sem=edge_recv.at[side, 1 - dt],
            device_id=(g + (1 if side else -1), t + dt),
            device_id_type=MESH,
        )

    lane = lanes_of()
    sub = lax.broadcasted_iota(jnp.int32, (8, LANES), 0)
    within = lane & 15
    shared = ((lane + EDGE) & 15) < 2 * EDGE
    cell_rows = cells_ref.reshape(2 * 2 * K * NYD, LANES)
    halo = 2 * K * NYD
    top, bottom = t == 0, t == tiles - 1

    def row_of(e):
        above = e < EDGE
        below = e >= EDGE + NYD
        where = jnp.where(above & ~top, 0, jnp.where(below & ~bottom, 2, 1))
        y = jnp.where(
            above,
            jnp.where(top, EDGE - 1 - e, e + NYD - EDGE),
            jnp.where(below & bottom, EDGE + 2 * NYD - 1 - e, e - EDGE - jnp.where(below, NYD, 0)),
        )
        return where, y

    row_at = [
        (1, e - EDGE) if EDGE <= e < EDGE + NYD else row_of(jnp.int32(e)) for e in range(EXT)
    ]

    def main_of(f, e, b):
        base = f * (K * NYD) + 64 * b
        where, y = row_at[e]
        if e < EDGE or e >= EDGE + NYD:
            base = base + jnp.where(where == 1, 0, halo)
        return cell_rows[pl.ds(base + y, 8, stride=NYD), :]

    def pack_coefs(e):
        where, y = row_at[e]
        source = 0 if isinstance(where, int) else jnp.where(where == 1, 0, 2 if e < EDGE else 1)
        rows = [jnp.broadcast_to(cf_ref[source, i, pl.ds(y, 1), :], (8, LANES)) for i in range(2)]
        block = jnp.where(sub == 0, rows[0], rows[1])
        block = jnp.where((lane < 8) | (lane >= LANES - 8), block, 0.0)
        for shift in (16, 32, 64):
            block = block + pltpu.roll(block, shift, 1)
        o_ref[e, COEF] = block
        own = rows[0]
        co_ref[0, 0, e] = (own + (1.0 - 4.0 * DIFFUSION)) * (1.0 / DIFFUSION)
        for s in range(1, STEPS + 1):
            co_ref[0, s, e] = rows[1] * ((1.0 - SLOW_RATE) ** (s - 1) / DIFFUSION**s)

    def send(c):
        for direction in range(2):
            @pl.when(has[1 if direction else -1])
            def _():
                for copy in row_copies(direction, c):
                    copy.start()

    def receive(c):
        for direction in range(2):
            @pl.when(has[-1 if direction else 1])
            def _():
                for copy in row_copies(direction, c):
                    copy.wait_recv()

    def settle(c):
        for direction in range(2):
            @pl.when(has[1 if direction else -1])
            def _():
                for copy in row_copies(direction, c):
                    copy.wait_send()

    for copy in cf_copies:
        copy.wait()
    wide_g = 1 + (g > 0).astype(jnp.int32) + (g < groups - 1).astype(jnp.int32)
    wide_t = 1 + (t > 0).astype(jnp.int32) + (t < tiles - 1).astype(jnp.int32)
    pl.semaphore_wait(barrier, wide_g * wide_t - 1 + len(greeted))

    for direction in range(2):
        @pl.when(has[1 if direction else -1])
        def _():
            cf_copy(direction).start()
    for group in range(GROUPS_K):
        local_copy(group).wait()
        for c in range(2 * group, min(2 * group + 2, WINDOW)):
            send(c)
    for y in range(NYD):
        pack_coefs(EDGE + y)
    for group in range(GROUPS_K):
        def pack_row(y, _):
            for f in range(2):
                packed = None
                for m in range(8):
                    block = cell_rows[pl.ds(f * (K * NYD) + 64 * (8 * group + m) + y, 8, stride=NYD), :]
                    if m == 0:
                        packed = block
                    else:
                        packed = jnp.where(
                            (lane >= 16 * m - 8) & (lane < 16 * m + 8), pltpu.roll(block, 16 * m, 1), packed
                        )
                o_ref[EDGE + y, f * (GROUPS_K + 1) + group] = packed
            return 0

        lax.fori_loop(0, NYD, pack_row, 0)

    def share_row(y, _):
        for i, (one, two) in enumerate(PAIRS):
            value = o_ref[EDGE + y, one]
            if two is not None:
                value = jnp.where(shared, value, pltpu.roll(o_ref[EDGE + y, two], 8, 1))
            t_ref[y, i] = value
        return 0

    lax.fori_loop(0, NYD, share_row, 0)

    for dt in (0, -1, 1):
        for side in range(2):
            @pl.when(exists(1 if side else -1, dt))
            def _():
                edge_copy(side, dt).start()
    for direction in range(2):
        @pl.when(has[-1 if direction else 1])
        def _():
            cf_copy(direction).wait_recv()
    for e in range(EXT):
        if e < EDGE or e >= EDGE + NYD:
            pack_coefs(e)

    def evolve(loads, coefs, stores):
        lots = range(len(loads))
        fast = [[[None] * EXT for _ in range(STEPS + 1)] for _ in lots]
        slow = [[[None] * EXT for _ in range(STEPS + 1)] for _ in lots]
        for e in range(EXT):
            for n in lots:
                fast[n][0][e] = loads[n](0, e)
                if 1 <= e < EXT - 1:
                    slow[n][0][e] = loads[n](1, e)
            for s in range(1, STEPS + 1):
                r = e - s
                if r < s or r > EXT - 1 - s:
                    continue
                drift = SLOW_RATE * DIFFUSION ** (s - 1) / (1.0 - SLOW_RATE) ** s
                for n in lots:
                    before = fast[n][s - 1]
                    old, old_slow = before[r], slow[n][s - 1][r]
                    total = (before[r - 1] + before[r + 1]) + (
                        pltpu.roll(old, 1, 1) + pltpu.roll(old, LANES - 1, 1)
                    )
                    new = total + (coefs[n](0, r) * old + coefs[n](s, r) * old_slow)
                    new_slow = old_slow + drift * old
                    fast[n][s][r] = new
                    slow[n][s][r] = new_slow
                    if s == STEPS:
                        stores[n](r - EDGE, new * DIFFUSION**STEPS)
                        stores[n](NYD + r - EDGE, new_slow * (1.0 - SLOW_RATE) ** STEPS)

    def block_steps(first):
        loads, stores = [], []
        for n in range(TOGETHER):
            b = first + n
            group = b // 8
            m = b - 8 * group
            rows = pl.ds(pl.multiple_of(8 * b, 8), 8)
            here = ((lane + 8) & (LANES - 1)) // 16 == m

            def load(f, e, b=b, group=group, m=m, here=here):
                value = main_of(f, e, b)
                if e < EDGE or e >= EDGE + NYD:
                    slot = f * (GROUPS_K + 1) + group
                    o_ref[e, slot] = jnp.where(here, pltpu.roll(value, 16 * m, 1), o_ref[e, slot])
                return value

            def store(fy, value, rows=rows):
                e_ref[fy, rows, :] = value

            loads.append(load)
            stores.append(store)
        evolve(loads, [lambda s, r: co_ref[0, s, r]] * TOGETHER, stores)

    def chunk(c, _):
        receive(c)

        @pl.when(c < CHUNKS - WINDOW)
        def _():
            send(c + WINDOW)

        def step(i, _):
            block_steps(PER_CHUNK * c + TOGETHER * i)
            return 0

        lax.fori_loop(0, PER_CHUNK // TOGETHER, step, 0)
        return 0

    lax.fori_loop(0, CHUNKS, chunk, 0)

    for dt in (0, -1, 1):
        for side in range(2):
            @pl.when(exists(-1 if side else 1, -dt))
            def _():
                edge_copy(side, dt).wait_recv()

    def join(side, e, slot, value):
        beside = within < EDGE if side == 0 else within >= 16 - EDGE
        q_ref[side, e, slot] = jnp.where(beside, value, o_ref[e, slot])

    for side in range(2):
        @pl.when(hasg[-1 if side else 1])
        def _():
            def join_row(k, _):
                for e in (4 * k, 4 * k + 1, 4 * k + 2, 4 * k + 3):
                    where, y = row_of(e)
                    for i, (one, two) in enumerate(PAIRS):
                        value = x_ref[side, where, y, i]
                        join(side, e, one, value)
                        if two is not None:
                            join(side, e, two, pltpu.roll(value, LANES - 8, 1))
                return 0

            lax.fori_loop(0, EXT // 4, join_row, 0)

        @pl.when(g == (0 if side else groups - 1))
        def _():
            def mirror_row(k, _):
                for e in (4 * k, 4 * k + 1, 4 * k + 2, 4 * k + 3):
                    for slot in range(SLOTS):
                        value = o_ref[e, slot]
                        flipped = None
                        for i in range(EDGE):
                            shift = LANES - 7 + 2 * i if side else 1 + 2 * i
                            moved = pltpu.roll(value, shift, 1)
                            flipped = moved if flipped is None else jnp.where((lane & 3) == i, moved, flipped)
                        join(side, e, slot, flipped)
                return 0

            lax.fori_loop(0, EXT // 4, mirror_row, 0)

    def side_coefs(k, _):
        for side, e in [(side, 2 * k - 1 + i) for side in range(2) for i in range(2)]:
            packed = q_ref[side, e, COEF]
            own = jnp.broadcast_to(packed[0:1, :], (8, LANES))
            cross = jnp.broadcast_to(packed[1:2, :], (8, LANES))
            co_ref[1 + side, 0, e] = (own + (1.0 - 4.0 * DIFFUSION)) * (1.0 / DIFFUSION)
            for s in range(1, STEPS + 1):
                co_ref[1 + side, s, e] = cross * ((1.0 - SLOW_RATE) ** (s - 1) / DIFFUSION**s)
        return 0

    lax.fori_loop(1, EXT // 2, side_coefs, 0)

    def side_step(group, _):
        loads, coefs, stores = [], [], []
        for side in range(2):
            loads.append(lambda f, e, side=side: q_ref[side, e, f * (GROUPS_K + 1) + group])
            coefs.append(lambda s, r, side=side: co_ref[1 + side, s, r])

            def store(fy, value, side=side):
                out_ref[side, fy, group] = value

            stores.append(store)
        evolve(loads, coefs, stores)
        return 0

    lax.fori_loop(0, GROUPS_K, side_step, 0)

    at_side = (lane < EDGE) | (lane >= LANES - EDGE)

    def merge(i, _):
        for fy in (4 * i, 4 * i + 1, 4 * i + 2, 4 * i + 3):
            for group in range(GROUPS_K):
                value = jnp.where(within < 8, out_ref[1, fy, group], out_ref[0, fy, group])
                for m in range(8):
                    rows = slice(64 * group + 8 * m, 64 * group + 8 * m + 8)
                    moved = pltpu.roll(value, LANES - 16 * m, 1) if m else value
                    e_ref[fy, rows, :] = jnp.where(at_side, moved, e_ref[fy, rows, :])
        return 0

    lax.fori_loop(0, NYD // 2, merge, 0)

    def drain():
        def finish(c, _):
            settle(c)
            return 0

        lax.fori_loop(0, CHUNKS, finish, 0)
        for dt in (0, -1, 1):
            for side in range(2):
                @pl.when(exists(1 if side else -1, dt))
                def _():
                    edge_copy(side, dt).wait_send()
        for direction in range(2):
            @pl.when(has[1 if direction else -1])
            def _():
                cf_copy(direction).wait_send()

    return drain


def eliminate(w_ref, emit, invert):
    lane = lanes_of()
    sub = lax.broadcasted_iota(jnp.int32, (8, LANES), 0)
    panels = K // 8
    for p in range(panels):
        j0 = 8 * p
        h, l0 = j0 // LANES, j0 % LANES
        halves = (0, 1) if invert else tuple(range(h, 2))
        inside = (lane >= l0) & (lane < l0 + 8)
        blk = {v: w_ref[j0 : j0 + 8, LANES * v : LANES * v + LANES] for v in halves}
        cols = [jnp.broadcast_to(blk[h][:, l0 + i : l0 + i + 1], (8, LANES)) for i in range(8)]
        el = [
            [jnp.broadcast_to(cols[i][m : m + 1, :], (8, LANES)) if m >= i else None for i in range(8)]
            for m in range(8)
        ]
        if invert:
            blk[h] = jnp.where(inside, jnp.where(lane - l0 == sub, 1.0, 0.0), blk[h])
        rows = {v: [jnp.broadcast_to(blk[v][m : m + 1, :], (8, LANES)) for m in range(8)] for v in halves}
        fac = [[None] * 8 for _ in range(8)]
        r, r2, pivots = [], [], []
        for i in range(8):
            pivots.append(el[i][i])
            r.append(lax.rsqrt(el[i][i]))
            r2.append(r[i] * r[i])
            for m in range(i + 1, 8):
                fac[m][i] = el[m][i] * r2[i]
            for k in range(i + 1, 8):
                for m in range(k, 8):
                    el[m][k] = el[m][k] - fac[k][i] * el[m][i]
            for v in halves:
                for m in range(i + 1, 8):
                    rows[v][m] = rows[v][m] - fac[m][i] * rows[v][i]
        for v in halves:
            out = rows[v][0] * r[0]
            for i in range(1, 8):
                out = jnp.where(sub == i, rows[v][i] * r[i], out)
            emit(p, v, out, lane, sub)
        emit(p, None, pivots, lane, sub)
        if p == panels - 1:
            break
        z = {v: [None] * 8 for v in halves}
        for v in halves:
            for i in range(7, -1, -1):
                acc = rows[v][i] * r2[i]
                for m in range(7, i, -1):
                    acc = acc - fac[m][i] * z[v][m]
                z[v][i] = acc
        for s in range(p + 1, panels):
            rng = slice(8 * s, 8 * s + 8)
            src = w_ref[rng, LANES * h : LANES * h + LANES]
            low = [jnp.broadcast_to(src[:, l0 + i : l0 + i + 1], (8, LANES)) for i in range(8)]
            for v in halves:
                if v == h:
                    cur = jnp.where(inside, 0.0, src) if invert else src
                else:
                    cur = w_ref[rng, LANES * v : LANES * v + LANES]
                a = low[0] * z[v][0]
                b = low[1] * z[v][1]
                for i in range(2, 8, 2):
                    a = a + low[i] * z[v][i]
                    b = b + low[i + 1] * z[v][i + 1]
                w_ref[rng, LANES * v : LANES * v + LANES] = cur - (a + b)
        yield


def split(a):
    high = a.astype(jnp.bfloat16)
    rest = a - high.astype(F32)
    middle = rest.astype(jnp.bfloat16)
    return high, middle, (rest - middle.astype(F32)).astype(jnp.bfloat16)


def gram_of(e_ref):
    def product(a, b):
        return lax.dot_general(a, b, (((1,), (1,)), ((), ())), preferred_element_type=F32)

    same = jnp.zeros((K, K), F32)
    mixed = jnp.zeros((K, K), F32)
    for y in range(NYD):
        a = jnp.concatenate([e_ref[y], e_ref[NYD + y]], axis=1)
        high, middle, low = split(a)
        same = same + product(high, high) + product(middle, middle)
        mixed = mixed + product(high, middle) + product(high, low)
    return same + mixed + jnp.transpose(mixed)


def tail_part(
    groups, tiles, line,
    e_ref, o_ref, r_ref,
    p_ref, near_ref, y_ref, z_ref, w_ref, sends, recvs,
):
    q, g, z, piece, inner, outer, in_line, in_y, in_z = line
    gram = gram_of(e_ref)
    w_ref[:, 0:LANES] = gram[:, 0:LANES]
    w_ref[:, LANES:K] = gram[:, LANES:K]
    w_ref[:, K : 2 * LANES] = jnp.zeros((K, 2 * LANES - K), F32)
    p_ref[0:64, :] = gram[0:64, 0:128]
    p_ref[64:128, :] = jnp.concatenate([gram[0:64, 128:192], gram[64:128, 64:128]], axis=1)
    p_ref[128:192, :] = jnp.concatenate([gram[64:128, 128:192], gram[128:192, 128:192]], axis=1)

    count = [0]

    def copy_to(src, dst, peer):
        i = count[0]
        count[0] += 1
        copy = pltpu.make_async_remote_copy(
            src_ref=src, dst_ref=dst, send_sem=sends.at[i], recv_sem=recvs.at[i],
            device_id=peer, device_id_type=MESH,
        )
        copy.start()
        return copy

    def rows(index):
        return pl.ds(pl.multiple_of(index * piece, 8), piece)

    def emit_factor(p, v, out, lane, sub):
        if v is None:
            return
        value = jnp.where(lane + LANES * v >= sub + 8 * p, out, 0.0)
        r_ref[8 * p : 8 * p + 8, LANES * v : LANES * v + LANES] = value

    r_ref[...] = jnp.zeros_like(r_ref)
    local = eliminate(w_ref, emit_factor, False)

    def advance(panels):
        for _ in range(panels):
            next(local, None)

    started = []
    phase = []
    for d in range(1, inner):
        phase.append(copy_to(p_ref.at[rows(lax.rem(q + d, inner))], near_ref.at[d - 1], in_line(d)))
    advance(6)
    total = p_ref[rows(q), :]
    for d, copy in enumerate(phase):
        copy.wait_recv()
        total = total + near_ref[d]
    started += phase
    for buf, me, size, peer_of in ((y_ref, g, groups, in_y), (z_ref, z, outer, in_z)):
        buf[me] = total
        phase = [copy_to(buf.at[me], buf.at[me], peer_of(d)) for d in range(1, size)]
        advance(5)
        for copy in phase:
            copy.wait_recv()
        total = buf[0]
        for i in range(1, size):
            total = total + buf[i]
        started += phase
    o_ref[rows(q), :] = total
    phase = [copy_to(o_ref.at[rows(q)], o_ref.at[rows(q)], in_line(d)) for d in range(1, inner)]
    advance(K // 8)
    for copy in phase:
        copy.wait_recv()
    started += phase
    for copy in started:
        copy.wait_send()


def solve_kernel(scale, o_ref, r_ref, c_ref, growth_ref, v_ref, inv_ref):
    u0, u1, u2 = o_ref[0:64, :], o_ref[64:128, :], o_ref[128:192, :]
    t0, t1, t2 = jnp.transpose(u0), jnp.transpose(u1), jnp.transpose(u2)
    v_ref[0:64, 0:LANES] = u0
    v_ref[0:64, LANES:] = u1
    v_ref[64:128, 0:LANES] = jnp.concatenate([t0[64:128], u1[:, 64:128]], axis=1)
    v_ref[64:128, LANES:] = u2
    v_ref[128:192, 0:LANES] = jnp.concatenate([t1[0:64], t2[0:64]], axis=1)
    v_ref[128:192, LANES:] = pltpu.roll(u2, 64, 1)
    diagonal = [jnp.ones((8, LANES), F32), jnp.ones((8, LANES), F32)]

    def emit_inverse(p, v, out, lane, sub):
        if v is None:
            h, l0 = 8 * p // LANES, 8 * p % LANES
            for i in range(8):
                diagonal[h] = jnp.where(lane == l0 + i, out[i], diagonal[h])
            return
        value = jnp.where(lane + LANES * v <= sub + 8 * p, out, 0.0)
        inv_ref[8 * p : 8 * p + 8, LANES * v : LANES * v + LANES] = value

    for _ in eliminate(v_ref, emit_inverse, True):
        pass
    growth_ref[0:1, 0:LANES] = 0.5 * jnp.log(diagonal[0][0:1, :])
    growth_ref[0:1, LANES:K] = 0.5 * jnp.log(diagonal[1][0:1, 0 : K - LANES])
    c_ref[...] = scale * lax.dot_general(
        r_ref[...], inv_ref[...], (((1,), (1,)), ((), ())),
        precision=lax.Precision.HIGHEST, preferred_element_type=F32,
    )


def main_kernel(groups, tiles, tan_hbm, self_hbm, cross_hbm, reduced_ref, factor_ref, e_ref, *scratch):
    g = lax.axis_index("grp")
    t = lax.axis_index("tile")
    inner = 8
    outer = tiles // inner
    piece = K // inner
    z = t // inner
    q = t - z * inner

    def in_line(d):
        return (g, z * inner + lax.rem(q + d, inner))

    def in_y(d):
        return (lax.rem(g + d, groups), t)

    def in_z(d):
        return (g, lax.rem(z + d, outer) * inner + q)

    peers = (
        [in_line(d) for d in range(1, inner)]
        + [in_y(d) for d in range(1, groups)]
        + [in_z(d) for d in range(1, outer)]
    )
    line = (q, g, z, piece, inner, outer, in_line, in_y, in_z)
    front_scratch, tail_scratch = scratch[:16], scratch[16:]
    drain = front_part(groups, tiles, peers, tan_hbm, self_hbm, cross_hbm, e_ref, *front_scratch)
    tail_part(groups, tiles, line, e_ref, reduced_ref, factor_ref, *tail_scratch)
    drain()


def run_main(groups, tiles, *arguments):
    hbm = pl.BlockSpec(memory_space=pltpu.HBM)
    copies = 2 * 7 + (groups - 1) + (tiles // 8 - 1)
    return pl.pallas_call(
        functools.partial(main_kernel, groups, tiles),
        out_shape=(jax.ShapeDtypeStruct((K, LANES), F32), jax.ShapeDtypeStruct((K, 2 * LANES), F32)),
        in_specs=[hbm] * 3,
        out_specs=[VMEM_SPEC] * 2,
        scratch_shapes=[
            pltpu.VMEM((2 * NYD, K, LANES), F32),
            pltpu.VMEM((2, 2, K, NYD, LANES), F32),
            pltpu.VMEM((3, 2, NYD, LANES), F32),
            pltpu.VMEM((EXT, SLOTS, 8, LANES), F32),
            pltpu.VMEM((NYD, len(PAIRS), 8, LANES), F32),
            pltpu.VMEM((2, 3, NYD, len(PAIRS), 8, LANES), F32),
            pltpu.VMEM((2, EXT, SLOTS, 8, LANES), F32),
            pltpu.VMEM((2, 2 * NYD, GROUPS_K, 8, LANES), F32),
            pltpu.VMEM((3, STEPS + 1, EXT, 8, LANES), F32),
            pltpu.SemaphoreType.DMA((GROUPS_K,)),
            pltpu.SemaphoreType.DMA((2,)),
            pltpu.SemaphoreType.DMA((2,)),
            pltpu.SemaphoreType.DMA((2,)),
            pltpu.SemaphoreType.DMA((2, CHUNKS, 2)),
            pltpu.SemaphoreType.DMA((2, CHUNKS, 2)),
            pltpu.SemaphoreType.DMA((2, 3)),
            pltpu.SemaphoreType.DMA((2, 3)),
            pltpu.VMEM((K, LANES), F32),
            pltpu.VMEM((7, K // 8, LANES), F32),
            pltpu.VMEM((groups, K // 8, LANES), F32),
            pltpu.VMEM((tiles // 8, K // 8, LANES), F32),
            pltpu.VMEM((K, 2 * LANES), F32),
            pltpu.SemaphoreType.DMA((copies,)),
            pltpu.SemaphoreType.DMA((copies,)),
        ],
        compiler_params=pltpu.CompilerParams(
            collective_id=0, has_side_effects=True, vmem_limit_bytes=LIMIT
        ),
        name="main",
    )(*[pltpu.with_memory_space_constraint(x, pltpu.HBM) for x in arguments])


def solve(scale, reduced, local_factor):
    return pl.pallas_call(
        functools.partial(solve_kernel, scale),
        out_shape=(jax.ShapeDtypeStruct((K, K), F32), jax.ShapeDtypeStruct((1, K), F32)),
        in_specs=[VMEM_SPEC] * 2,
        out_specs=[VMEM_SPEC] * 2,
        scratch_shapes=[pltpu.VMEM((K, 2 * LANES), F32)] * 2,
        compiler_params=pltpu.CompilerParams(vmem_limit_bytes=LIMIT),
        name="solve",
    )(reduced, local_factor)


def per_device(groups, tiles, tangents, reaction_self, reaction_cross):
    reduced, local_factor = run_main(groups, tiles, tangents, reaction_self, reaction_cross)
    corrections, growth = solve(math.sqrt(groups * tiles), reduced, local_factor)
    return (corrections, growth.reshape(K))


def solution(mesh):
    groups, tiles = mesh.shape["grp"], mesh.shape["tile"]
    in_specs = (P(None, None, "tile", "grp"), P("tile", "grp"), P("tile", "grp"))
    out_specs = (P(("grp", "tile"), None), P())
    return jax.shard_map(
        functools.partial(per_device, groups, tiles),
        mesh=mesh, in_specs=in_specs, out_specs=out_specs, check_vma=False,
    )
```

```python
import functools
import math

import jax
import jax.numpy as jnp
from jax import lax
from jax.experimental import pallas as pl
from jax.experimental.pallas import tpu as pltpu
from jax.sharding import PartitionSpec as P

MESH = pl.DeviceIdType.MESH
F32 = jnp.float32
STEPS = 4
K = 192
NYD = 8
LANES = 128
BLOCKS_K = K // 8
GROUPS_K = BLOCKS_K // 8
PER_CHUNK = 4
CHUNKS = BLOCKS_K // PER_CHUNK
CHUNK = 8 * PER_CHUNK
WINDOW = 6
TOGETHER = 2
COEF = GROUPS_K
SLOTS = 2 * GROUPS_K + 1
PAIRS = ((0, 1), (2, 6), (4, 5), (COEF, None))
EDGE = STEPS
EXT = NYD + 2 * EDGE
DIFFUSION = 0.2
SLOW_RATE = 0.05
LIMIT = 20 << 20
VMEM_SPEC = pl.BlockSpec(memory_space=pltpu.VMEM)
NEIGHBOURS = [(dg, dt) for dg in (-1, 0, 1) for dt in (-1, 0, 1) if (dg, dt) != (0, 0)]


def lanes_of(shape=(8, LANES)):
    return lax.broadcasted_iota(jnp.int32, shape, 1)


def front_part(
    groups, tiles, greeted,
    tan_hbm, self_hbm, cross_hbm, e_ref,
    cells_ref, cf_ref, o_ref, t_ref, x_ref, q_ref, out_ref, co_ref,
    local_sem, cf_sem, cf_send, cf_recv, row_send, row_recv, edge_send, edge_recv,
):
    g = lax.axis_index("grp")
    t = lax.axis_index("tile")
    has = {-1: t > 0, 0: None, 1: t < tiles - 1}
    hasg = {-1: g > 0, 0: None, 1: g < groups - 1}

    def exists(dg, dt):
        terms = [c for c in (hasg[dg], has[dt]) if c is not None]
        return terms[0] if len(terms) == 1 else terms[0] & terms[1]

    barrier = pltpu.get_barrier_semaphore()
    for dg, dt in NEIGHBOURS:
        @pl.when(exists(dg, dt))
        def _():
            pl.semaphore_signal(barrier, inc=1, device_id=(g + dg, t + dt), device_id_type=MESH)
    for peer in greeted:
        pl.semaphore_signal(barrier, inc=1, device_id=peer, device_id_type=MESH)

    def fields_of(c):
        return pl.ds(c * CHUNK if isinstance(c, int) else pl.multiple_of(c * CHUNK, 8), CHUNK)

    def local_copy(group):
        fields = pl.ds(64 * group, 64)
        return pltpu.make_async_copy(tan_hbm.at[:, fields], cells_ref.at[0, :, fields], local_sem.at[group])

    cf_copies = [
        pltpu.make_async_copy(src, cf_ref.at[0, i], cf_sem.at[i]) for i, src in enumerate((self_hbm, cross_hbm))
    ]
    for copy in cf_copies:
        copy.start()
    for group in range(GROUPS_K):
        local_copy(group).start()

    def row_copies(direction, c):
        fields = fields_of(c)
        spans = (slice(0, 4), slice(0, 3)) if direction == 0 else (slice(4, 8), slice(5, 8))
        return [
            pltpu.make_async_remote_copy(
                src_ref=cells_ref.at[0, f, fields, spans[f], :],
                dst_ref=cells_ref.at[1, f, fields, spans[f], :],
                send_sem=row_send.at[direction, c, f],
                recv_sem=row_recv.at[direction, c, f],
                device_id=(g, t + (1 if direction else -1)),
                device_id_type=MESH,
            )
            for f in range(2)
        ]

    def cf_copy(direction):
        return pltpu.make_async_remote_copy(
            src_ref=cf_ref.at[0],
            dst_ref=cf_ref.at[1 + direction],
            send_sem=cf_send.at[direction],
            recv_sem=cf_recv.at[direction],
            device_id=(g, t + (1 if direction else -1)),
            device_id_type=MESH,
        )

    def edge_copy(side, dt):
        rows = {-1: slice(0, 4), 0: slice(0, 8), 1: slice(4, 8)}[dt]
        return pltpu.make_async_remote_copy(
            src_ref=t_ref.at[rows],
            dst_ref=x_ref.at[side, 1 - dt, rows],
            send_sem=edge_send.at[side, 1 - dt],
            recv_sem=edge_recv.at[side, 1 - dt],
            device_id=(g + (1 if side else -1), t + dt),
            device_id_type=MESH,
        )

    lane = lanes_of()
    sub = lax.broadcasted_iota(jnp.int32, (8, LANES), 0)
    within = lane & 15
    shared = ((lane + EDGE) & 15) < 2 * EDGE
    cell_rows = cells_ref.reshape(2 * 2 * K * NYD, LANES)
    halo = 2 * K * NYD
    top, bottom = t == 0, t == tiles - 1

    def row_of(e):
        above = e < EDGE
        below = e >= EDGE + NYD
        where = jnp.where(above & ~top, 0, jnp.where(below & ~bottom, 2, 1))
        y = jnp.where(
            above,
            jnp.where(top, EDGE - 1 - e, e + NYD - EDGE),
            jnp.where(below & bottom, EDGE + 2 * NYD - 1 - e, e - EDGE - jnp.where(below, NYD, 0)),
        )
        return where, y

    row_at = [
        (1, e - EDGE) if EDGE <= e < EDGE + NYD else row_of(jnp.int32(e)) for e in range(EXT)
    ]

    def main_of(f, e, b):
        base = f * (K * NYD) + 64 * b
        where, y = row_at[e]
        if e < EDGE or e >= EDGE + NYD:
            base = base + jnp.where(where == 1, 0, halo)
        return cell_rows[pl.ds(base + y, 8, stride=NYD), :]

    def pack_coefs(e):
        where, y = row_at[e]
        source = 0 if isinstance(where, int) else jnp.where(where == 1, 0, 2 if e < EDGE else 1)
        rows = [jnp.broadcast_to(cf_ref[source, i, pl.ds(y, 1), :], (8, LANES)) for i in range(2)]
        block = jnp.where(sub == 0, rows[0], rows[1])
        block = jnp.where((lane < 8) | (lane >= LANES - 8), block, 0.0)
        for shift in (16, 32, 64):
            block = block + pltpu.roll(block, shift, 1)
        o_ref[e, COEF] = block
        own = rows[0]
        co_ref[0, 0, e] = (own + (1.0 - 4.0 * DIFFUSION)) * (1.0 / DIFFUSION)
        for s in range(1, STEPS + 1):
            co_ref[0, s, e] = rows[1] * ((1.0 - SLOW_RATE) ** (s - 1) / DIFFUSION**s)

    def send(c):
        for direction in range(2):
            @pl.when(has[1 if direction else -1])
            def _():
                for copy in row_copies(direction, c):
                    copy.start()

    def receive(c):
        for direction in range(2):
            @pl.when(has[-1 if direction else 1])
            def _():
                for copy in row_copies(direction, c):
                    copy.wait_recv()

    def settle(c):
        for direction in range(2):
            @pl.when(has[1 if direction else -1])
            def _():
                for copy in row_copies(direction, c):
                    copy.wait_send()

    for copy in cf_copies:
        copy.wait()
    wide_g = 1 + (g > 0).astype(jnp.int32) + (g < groups - 1).astype(jnp.int32)
    wide_t = 1 + (t > 0).astype(jnp.int32) + (t < tiles - 1).astype(jnp.int32)
    pl.semaphore_wait(barrier, wide_g * wide_t - 1 + len(greeted))

    for direction in range(2):
        @pl.when(has[1 if direction else -1])
        def _():
            cf_copy(direction).start()
    for group in range(GROUPS_K):
        local_copy(group).wait()
        for c in range(2 * group, min(2 * group + 2, WINDOW)):
            send(c)
    for y in range(NYD):
        pack_coefs(EDGE + y)
    for group in range(GROUPS_K):
        def pack_row(y, _):
            for f in range(2):
                packed = None
                for m in range(8):
                    block = cell_rows[pl.ds(f * (K * NYD) + 64 * (8 * group + m) + y, 8, stride=NYD), :]
                    if m == 0:
                        packed = block
                    else:
                        packed = jnp.where(
                            (lane >= 16 * m - 8) & (lane < 16 * m + 8), pltpu.roll(block, 16 * m, 1), packed
                        )
                o_ref[EDGE + y, f * (GROUPS_K + 1) + group] = packed
            return 0

        lax.fori_loop(0, NYD, pack_row, 0)

    def share_row(y, _):
        for i, (one, two) in enumerate(PAIRS):
            value = o_ref[EDGE + y, one]
            if two is not None:
                value = jnp.where(shared, value, pltpu.roll(o_ref[EDGE + y, two], 8, 1))
            t_ref[y, i] = value
        return 0

    lax.fori_loop(0, NYD, share_row, 0)

    for dt in (0, -1, 1):
        for side in range(2):
            @pl.when(exists(1 if side else -1, dt))
            def _():
                edge_copy(side, dt).start()
    for direction in range(2):
        @pl.when(has[-1 if direction else 1])
        def _():
            cf_copy(direction).wait_recv()
    for e in range(EXT):
        if e < EDGE or e >= EDGE + NYD:
            pack_coefs(e)

    def evolve(loads, coefs, stores):
        lots = range(len(loads))
        fast = [[[None] * EXT for _ in range(STEPS + 1)] for _ in lots]
        slow = [[[None] * EXT for _ in range(STEPS + 1)] for _ in lots]
        for e in range(EXT):
            for n in lots:
                fast[n][0][e] = loads[n](0, e)
                if 1 <= e < EXT - 1:
                    slow[n][0][e] = loads[n](1, e)
            for s in range(1, STEPS + 1):
                r = e - s
                if r < s or r > EXT - 1 - s:
                    continue
                drift = SLOW_RATE * DIFFUSION ** (s - 1) / (1.0 - SLOW_RATE) ** s
                for n in lots:
                    before = fast[n][s - 1]
                    old, old_slow = before[r], slow[n][s - 1][r]
                    total = (before[r - 1] + before[r + 1]) + (
                        pltpu.roll(old, 1, 1) + pltpu.roll(old, LANES - 1, 1)
                    )
                    new = total + (coefs[n](0, r) * old + coefs[n](s, r) * old_slow)
                    new_slow = old_slow + drift * old
                    fast[n][s][r] = new
                    slow[n][s][r] = new_slow
                    if s == STEPS:
                        stores[n](r - EDGE, new * DIFFUSION**STEPS)
                        stores[n](NYD + r - EDGE, new_slow * (1.0 - SLOW_RATE) ** STEPS)

    def block_steps(first):
        loads, stores = [], []
        for n in range(TOGETHER):
            b = first + n
            group = b // 8
            m = b - 8 * group
            rows = pl.ds(pl.multiple_of(8 * b, 8), 8)
            here = ((lane + 8) & (LANES - 1)) // 16 == m

            def load(f, e, b=b, group=group, m=m, here=here):
                value = main_of(f, e, b)
                if e < EDGE or e >= EDGE + NYD:
                    slot = f * (GROUPS_K + 1) + group
                    o_ref[e, slot] = jnp.where(here, pltpu.roll(value, 16 * m, 1), o_ref[e, slot])
                return value

            def store(fy, value, rows=rows):
                e_ref[fy, rows, :] = value

            loads.append(load)
            stores.append(store)
        evolve(loads, [lambda s, r: co_ref[0, s, r]] * TOGETHER, stores)

    def chunk(c, _):
        receive(c)

        @pl.when(c < CHUNKS - WINDOW)
        def _():
            send(c + WINDOW)

        def step(i, _):
            block_steps(PER_CHUNK * c + TOGETHER * i)
            return 0

        lax.fori_loop(0, PER_CHUNK // TOGETHER, step, 0)
        return 0

    lax.fori_loop(0, CHUNKS, chunk, 0)

    for dt in (0, -1, 1):
        for side in range(2):
            @pl.when(exists(-1 if side else 1, -dt))
            def _():
                edge_copy(side, dt).wait_recv()

    def join(side, e, slot, value):
        beside = within < EDGE if side == 0 else within >= 16 - EDGE
        q_ref[side, e, slot] = jnp.where(beside, value, o_ref[e, slot])

    for side in range(2):
        @pl.when(hasg[-1 if side else 1])
        def _():
            def join_row(k, _):
                for e in (4 * k, 4 * k + 1, 4 * k + 2, 4 * k + 3):
                    where, y = row_of(e)
                    for i, (one, two) in enumerate(PAIRS):
                        value = x_ref[side, where, y, i]
                        join(side, e, one, value)
                        if two is not None:
                            join(side, e, two, pltpu.roll(value, LANES - 8, 1))
                return 0

            lax.fori_loop(0, EXT // 4, join_row, 0)

        @pl.when(g == (0 if side else groups - 1))
        def _():
            def mirror_row(k, _):
                for e in (4 * k, 4 * k + 1, 4 * k + 2, 4 * k + 3):
                    for slot in range(SLOTS):
                        value = o_ref[e, slot]
                        flipped = None
                        for i in range(EDGE):
                            shift = LANES - 7 + 2 * i if side else 1 + 2 * i
                            moved = pltpu.roll(value, shift, 1)
                            flipped = moved if flipped is None else jnp.where((lane & 3) == i, moved, flipped)
                        join(side, e, slot, flipped)
                return 0

            lax.fori_loop(0, EXT // 4, mirror_row, 0)

    def side_coefs(k, _):
        for side, e in [(side, 2 * k - 1 + i) for side in range(2) for i in range(2)]:
            packed = q_ref[side, e, COEF]
            own = jnp.broadcast_to(packed[0:1, :], (8, LANES))
            cross = jnp.broadcast_to(packed[1:2, :], (8, LANES))
            co_ref[1 + side, 0, e] = (own + (1.0 - 4.0 * DIFFUSION)) * (1.0 / DIFFUSION)
            for s in range(1, STEPS + 1):
                co_ref[1 + side, s, e] = cross * ((1.0 - SLOW_RATE) ** (s - 1) / DIFFUSION**s)
        return 0

    lax.fori_loop(1, EXT // 2, side_coefs, 0)

    def side_step(group, _):
        loads, coefs, stores = [], [], []
        for side in range(2):
            loads.append(lambda f, e, side=side: q_ref[side, e, f * (GROUPS_K + 1) + group])
            coefs.append(lambda s, r, side=side: co_ref[1 + side, s, r])

            def store(fy, value, side=side):
                out_ref[side, fy, group] = value

            stores.append(store)
        evolve(loads, coefs, stores)
        return 0

    lax.fori_loop(0, GROUPS_K, side_step, 0)

    at_side = (lane < EDGE) | (lane >= LANES - EDGE)

    def merge(i, _):
        for fy in (4 * i, 4 * i + 1, 4 * i + 2, 4 * i + 3):
            for group in range(GROUPS_K):
                value = jnp.where(within < 8, out_ref[1, fy, group], out_ref[0, fy, group])
                for m in range(8):
                    rows = slice(64 * group + 8 * m, 64 * group + 8 * m + 8)
                    moved = pltpu.roll(value, LANES - 16 * m, 1) if m else value
                    e_ref[fy, rows, :] = jnp.where(at_side, moved, e_ref[fy, rows, :])
        return 0

    lax.fori_loop(0, NYD // 2, merge, 0)

    def drain():
        def finish(c, _):
            settle(c)
            return 0

        lax.fori_loop(0, CHUNKS, finish, 0)
        for dt in (0, -1, 1):
            for side in range(2):
                @pl.when(exists(1 if side else -1, dt))
                def _():
                    edge_copy(side, dt).wait_send()
        for direction in range(2):
            @pl.when(has[1 if direction else -1])
            def _():
                cf_copy(direction).wait_send()

    return drain


def eliminate(w_ref, emit, invert):
    lane = lanes_of()
    sub = lax.broadcasted_iota(jnp.int32, (8, LANES), 0)
    panels = K // 8
    for p in range(panels):
        j0 = 8 * p
        h, l0 = j0 // LANES, j0 % LANES
        halves = (0, 1) if invert else tuple(range(h, 2))
        inside = (lane >= l0) & (lane < l0 + 8)
        blk = {v: w_ref[j0 : j0 + 8, LANES * v : LANES * v + LANES] for v in halves}
        cols = [jnp.broadcast_to(blk[h][:, l0 + i : l0 + i + 1], (8, LANES)) for i in range(8)]
        el = [
            [jnp.broadcast_to(cols[i][m : m + 1, :], (8, LANES)) if m >= i else None for i in range(8)]
            for m in range(8)
        ]
        if invert:
            blk[h] = jnp.where(inside, jnp.where(lane - l0 == sub, 1.0, 0.0), blk[h])
        rows = {v: [jnp.broadcast_to(blk[v][m : m + 1, :], (8, LANES)) for m in range(8)] for v in halves}
        fac = [[None] * 8 for _ in range(8)]
        r, r2, pivots = [], [], []
        for i in range(8):
            pivots.append(el[i][i])
            r.append(lax.rsqrt(el[i][i]))
            r2.append(r[i] * r[i])
            for m in range(i + 1, 8):
                fac[m][i] = el[m][i] * r2[i]
            for k in range(i + 1, 8):
                for m in range(k, 8):
                    el[m][k] = el[m][k] - fac[k][i] * el[m][i]
            for v in halves:
                for m in range(i + 1, 8):
                    rows[v][m] = rows[v][m] - fac[m][i] * rows[v][i]
        for v in halves:
            out = rows[v][0] * r[0]
            for i in range(1, 8):
                out = jnp.where(sub == i, rows[v][i] * r[i], out)
            emit(p, v, out, lane, sub)
        emit(p, None, pivots, lane, sub)
        if p == panels - 1:
            break
        z = {v: [None] * 8 for v in halves}
        for v in halves:
            for i in range(7, -1, -1):
                acc = rows[v][i] * r2[i]
                for m in range(7, i, -1):
                    acc = acc - fac[m][i] * z[v][m]
                z[v][i] = acc
        for s in range(p + 1, panels):
            rng = slice(8 * s, 8 * s + 8)
            src = w_ref[rng, LANES * h : LANES * h + LANES]
            low = [jnp.broadcast_to(src[:, l0 + i : l0 + i + 1], (8, LANES)) for i in range(8)]
            for v in halves:
                if v == h:
                    cur = jnp.where(inside, 0.0, src) if invert else src
                else:
                    cur = w_ref[rng, LANES * v : LANES * v + LANES]
                a = low[0] * z[v][0]
                b = low[1] * z[v][1]
                for i in range(2, 8, 2):
                    a = a + low[i] * z[v][i]
                    b = b + low[i + 1] * z[v][i + 1]
                w_ref[rng, LANES * v : LANES * v + LANES] = cur - (a + b)
        yield


def split(a):
    high = a.astype(jnp.bfloat16)
    rest = a - high.astype(F32)
    middle = rest.astype(jnp.bfloat16)
    return high, middle, (rest - middle.astype(F32)).astype(jnp.bfloat16)


def gram_of(e_ref):
    def product(a, b):
        return lax.dot_general(a, b, (((1,), (1,)), ((), ())), preferred_element_type=F32)

    same = jnp.zeros((K, K), F32)
    mixed = jnp.zeros((K, K), F32)
    for y in range(NYD):
        a = jnp.concatenate([e_ref[y], e_ref[NYD + y]], axis=1)
        high, middle, low = split(a)
        same = same + product(high, high) + product(middle, middle)
        mixed = mixed + product(high, middle) + product(high, low)
    return same + mixed + jnp.transpose(mixed)


def tail_part(
    groups, tiles, line,
    e_ref, o_ref, r_ref,
    p_ref, near_ref, y_ref, z_ref, w_ref, sends, recvs,
):
    q, g, z, piece, inner, outer, in_line, in_y, in_z = line
    gram = gram_of(e_ref)
    w_ref[:, 0:LANES] = gram[:, 0:LANES]
    w_ref[:, LANES:K] = gram[:, LANES:K]
    w_ref[:, K : 2 * LANES] = jnp.zeros((K, 2 * LANES - K), F32)
    p_ref[0:64, :] = gram[0:64, 0:128]
    p_ref[64:128, :] = jnp.concatenate([gram[0:64, 128:192], gram[64:128, 64:128]], axis=1)
    p_ref[128:192, :] = jnp.concatenate([gram[64:128, 128:192], gram[128:192, 128:192]], axis=1)

    count = [0]

    def copy_to(src, dst, peer):
        i = count[0]
        count[0] += 1
        copy = pltpu.make_async_remote_copy(
            src_ref=src, dst_ref=dst, send_sem=sends.at[i], recv_sem=recvs.at[i],
            device_id=peer, device_id_type=MESH,
        )
        copy.start()
        return copy

    def rows(index):
        return pl.ds(pl.multiple_of(index * piece, 8), piece)

    def emit_factor(p, v, out, lane, sub):
        if v is None:
            return
        value = jnp.where(lane + LANES * v >= sub + 8 * p, out, 0.0)
        r_ref[8 * p : 8 * p + 8, LANES * v : LANES * v + LANES] = value

    r_ref[...] = jnp.zeros_like(r_ref)
    local = eliminate(w_ref, emit_factor, False)

    def advance(panels):
        for _ in range(panels):
            next(local, None)

    started = []
    phase = []
    for d in range(1, inner):
        phase.append(copy_to(p_ref.at[rows(lax.rem(q + d, inner))], near_ref.at[d - 1], in_line(d)))
    advance(6)
    total = p_ref[rows(q), :]
    for d, copy in enumerate(phase):
        copy.wait_recv()
        total = total + near_ref[d]
    started += phase
    for buf, me, size, peer_of in ((y_ref, g, groups, in_y), (z_ref, z, outer, in_z)):
        buf[me] = total
        phase = [copy_to(buf.at[me], buf.at[me], peer_of(d)) for d in range(1, size)]
        advance(5)
        for copy in phase:
            copy.wait_recv()
        total = buf[0]
        for i in range(1, size):
            total = total + buf[i]
        started += phase
    o_ref[rows(q), :] = total
    phase = [copy_to(o_ref.at[rows(q)], o_ref.at[rows(q)], in_line(d)) for d in range(1, inner)]
    advance(K // 8)
    for copy in phase:
        copy.wait_recv()
    started += phase
    for copy in started:
        copy.wait_send()


def solve_kernel(scale, o_ref, r_ref, c_ref, growth_ref, v_ref, inv_ref):
    u0, u1, u2 = o_ref[0:64, :], o_ref[64:128, :], o_ref[128:192, :]
    t0, t1, t2 = jnp.transpose(u0), jnp.transpose(u1), jnp.transpose(u2)
    v_ref[0:64, 0:LANES] = u0
    v_ref[0:64, LANES:] = u1
    v_ref[64:128, 0:LANES] = jnp.concatenate([t0[64:128], u1[:, 64:128]], axis=1)
    v_ref[64:128, LANES:] = u2
    v_ref[128:192, 0:LANES] = jnp.concatenate([t1[0:64], t2[0:64]], axis=1)
    v_ref[128:192, LANES:] = pltpu.roll(u2, 64, 1)
    diagonal = [jnp.ones((8, LANES), F32), jnp.ones((8, LANES), F32)]

    def emit_inverse(p, v, out, lane, sub):
        if v is None:
            h, l0 = 8 * p // LANES, 8 * p % LANES
            for i in range(8):
                diagonal[h] = jnp.where(lane == l0 + i, out[i], diagonal[h])
            return
        value = jnp.where(lane + LANES * v <= sub + 8 * p, out, 0.0)
        inv_ref[8 * p : 8 * p + 8, LANES * v : LANES * v + LANES] = value

    for _ in eliminate(v_ref, emit_inverse, True):
        pass
    growth_ref[0:1, 0:LANES] = 0.5 * jnp.log(diagonal[0][0:1, :])
    growth_ref[0:1, LANES:K] = 0.5 * jnp.log(diagonal[1][0:1, 0 : K - LANES])
    c_ref[...] = scale * lax.dot_general(
        r_ref[...], inv_ref[...], (((1,), (1,)), ((), ())),
        precision=lax.Precision.HIGHEST, preferred_element_type=F32,
    )


def main_kernel(groups, tiles, tan_hbm, self_hbm, cross_hbm, reduced_ref, factor_ref, e_ref, *scratch):
    g = lax.axis_index("grp")
    t = lax.axis_index("tile")
    inner = 8
    outer = tiles // inner
    piece = K // inner
    z = t // inner
    q = t - z * inner

    def in_line(d):
        return (g, z * inner + lax.rem(q + d, inner))

    def in_y(d):
        return (lax.rem(g + d, groups), t)

    def in_z(d):
        return (g, lax.rem(z + d, outer) * inner + q)

    peers = (
        [in_line(d) for d in range(1, inner)]
        + [in_y(d) for d in range(1, groups)]
        + [in_z(d) for d in range(1, outer)]
    )
    line = (q, g, z, piece, inner, outer, in_line, in_y, in_z)
    front_scratch, tail_scratch = scratch[:16], scratch[16:]
    drain = front_part(groups, tiles, peers, tan_hbm, self_hbm, cross_hbm, e_ref, *front_scratch)
    tail_part(groups, tiles, line, e_ref, reduced_ref, factor_ref, *tail_scratch)
    drain()


def run_main(groups, tiles, *arguments):
    hbm = pl.BlockSpec(memory_space=pltpu.HBM)
    copies = 2 * 7 + (groups - 1) + (tiles // 8 - 1)
    return pl.pallas_call(
        functools.partial(main_kernel, groups, tiles),
        out_shape=(jax.ShapeDtypeStruct((K, LANES), F32), jax.ShapeDtypeStruct((K, 2 * LANES), F32)),
        in_specs=[hbm] * 3,
        out_specs=[VMEM_SPEC] * 2,
        scratch_shapes=[
            pltpu.VMEM((2 * NYD, K, LANES), F32),
            pltpu.VMEM((2, 2, K, NYD, LANES), F32),
            pltpu.VMEM((3, 2, NYD, LANES), F32),
            pltpu.VMEM((EXT, SLOTS, 8, LANES), F32),
            pltpu.VMEM((NYD, len(PAIRS), 8, LANES), F32),
            pltpu.VMEM((2, 3, NYD, len(PAIRS), 8, LANES), F32),
            pltpu.VMEM((2, EXT, SLOTS, 8, LANES), F32),
            pltpu.VMEM((2, 2 * NYD, GROUPS_K, 8, LANES), F32),
            pltpu.VMEM((3, STEPS + 1, EXT, 8, LANES), F32),
            pltpu.SemaphoreType.DMA((GROUPS_K,)),
            pltpu.SemaphoreType.DMA((2,)),
            pltpu.SemaphoreType.DMA((2,)),
            pltpu.SemaphoreType.DMA((2,)),
            pltpu.SemaphoreType.DMA((2, CHUNKS, 2)),
            pltpu.SemaphoreType.DMA((2, CHUNKS, 2)),
            pltpu.SemaphoreType.DMA((2, 3)),
            pltpu.SemaphoreType.DMA((2, 3)),
            pltpu.VMEM((K, LANES), F32),
            pltpu.VMEM((7, K // 8, LANES), F32),
            pltpu.VMEM((groups, K // 8, LANES), F32),
            pltpu.VMEM((tiles // 8, K // 8, LANES), F32),
            pltpu.VMEM((K, 2 * LANES), F32),
            pltpu.SemaphoreType.DMA((copies,)),
            pltpu.SemaphoreType.DMA((copies,)),
        ],
        compiler_params=pltpu.CompilerParams(
            collective_id=0, has_side_effects=True, vmem_limit_bytes=LIMIT
        ),
        name="main",
    )(*[pltpu.with_memory_space_constraint(x, pltpu.HBM) for x in arguments])


def solve(scale, reduced, local_factor):
    return pl.pallas_call(
        functools.partial(solve_kernel, scale),
        out_shape=(jax.ShapeDtypeStruct((K, K), F32), jax.ShapeDtypeStruct((1, K), F32)),
        in_specs=[VMEM_SPEC] * 2,
        out_specs=[VMEM_SPEC] * 2,
        scratch_shapes=[pltpu.VMEM((K, 2 * LANES), F32)] * 2,
        compiler_params=pltpu.CompilerParams(vmem_limit_bytes=LIMIT),
        name="solve",
    )(reduced, local_factor)


def per_device(groups, tiles, tangents, reaction_self, reaction_cross):
    reduced, local_factor = run_main(groups, tiles, tangents, reaction_self, reaction_cross)
    corrections, growth = solve(math.sqrt(groups * tiles), reduced, local_factor)
    return (corrections, growth.reshape(K))


def solution(mesh):
    groups, tiles = mesh.shape["grp"], mesh.shape["tile"]
    in_specs = (P(None, None, "tile", "grp"), P("tile", "grp"), P("tile", "grp"))
    out_specs = (P(("grp", "tile"), None), P())
    return jax.shard_map(
        functools.partial(per_device, groups, tiles),
        mesh=mesh, in_specs=in_specs, out_specs=out_specs, check_vma=False,
    )
```

```python
import functools
import math

import jax
import jax.numpy as jnp
from jax import lax
from jax.experimental import pallas as pl
from jax.experimental.pallas import tpu as pltpu
from jax.sharding import PartitionSpec as P

MESH = pl.DeviceIdType.MESH
F32 = jnp.float32
STEPS = 4
K = 192
NYD = 8
LANES = 128
BLOCKS_K = K // 8
GROUPS_K = BLOCKS_K // 8
PER_CHUNK = 4
CHUNKS = BLOCKS_K // PER_CHUNK
CHUNK = 8 * PER_CHUNK
WINDOW = 6
TOGETHER = 2
COEF = GROUPS_K
SLOTS = 2 * GROUPS_K + 1
PAIRS = ((0, 1), (2, 6), (4, 5), (COEF, None))
EDGE = STEPS
EXT = NYD + 2 * EDGE
DIFFUSION = 0.2
SLOW_RATE = 0.05
LIMIT = 20 << 20
VMEM_SPEC = pl.BlockSpec(memory_space=pltpu.VMEM)
NEIGHBOURS = [(dg, dt) for dg in (-1, 0, 1) for dt in (-1, 0, 1) if (dg, dt) != (0, 0)]


def lanes_of(shape=(8, LANES)):
    return lax.broadcasted_iota(jnp.int32, shape, 1)


def front_part(
    groups, tiles, greeted,
    tan_hbm, self_hbm, cross_hbm, e_ref,
    cells_ref, cf_ref, o_ref, t_ref, x_ref, q_ref, out_ref, co_ref,
    local_sem, cf_sem, cf_send, cf_recv, row_send, row_recv, edge_send, edge_recv,
):
    g = lax.axis_index("grp")
    t = lax.axis_index("tile")
    has = {-1: t > 0, 0: None, 1: t < tiles - 1}
    hasg = {-1: g > 0, 0: None, 1: g < groups - 1}

    def exists(dg, dt):
        terms = [c for c in (hasg[dg], has[dt]) if c is not None]
        return terms[0] if len(terms) == 1 else terms[0] & terms[1]

    barrier = pltpu.get_barrier_semaphore()
    for dg, dt in NEIGHBOURS:
        @pl.when(exists(dg, dt))
        def _():
            pl.semaphore_signal(barrier, inc=1, device_id=(g + dg, t + dt), device_id_type=MESH)
    for peer in greeted:
        pl.semaphore_signal(barrier, inc=1, device_id=peer, device_id_type=MESH)

    def fields_of(c):
        return pl.ds(c * CHUNK if isinstance(c, int) else pl.multiple_of(c * CHUNK, 8), CHUNK)

    def local_copy(group):
        fields = pl.ds(64 * group, 64)
        return pltpu.make_async_copy(tan_hbm.at[:, fields], cells_ref.at[0, :, fields], local_sem.at[group])

    cf_copies = [
        pltpu.make_async_copy(src, cf_ref.at[0, i], cf_sem.at[i]) for i, src in enumerate((self_hbm, cross_hbm))
    ]
    for copy in cf_copies:
        copy.start()
    for group in range(GROUPS_K):
        local_copy(group).start()

    def row_copies(direction, c):
        fields = fields_of(c)
        spans = (slice(0, 4), slice(0, 3)) if direction == 0 else (slice(4, 8), slice(5, 8))
        return [
            pltpu.make_async_remote_copy(
                src_ref=cells_ref.at[0, f, fields, spans[f], :],
                dst_ref=cells_ref.at[1, f, fields, spans[f], :],
                send_sem=row_send.at[direction, c, f],
                recv_sem=row_recv.at[direction, c, f],
                device_id=(g, t + (1 if direction else -1)),
                device_id_type=MESH,
            )
            for f in range(2)
        ]

    def cf_copy(direction):
        return pltpu.make_async_remote_copy(
            src_ref=cf_ref.at[0],
            dst_ref=cf_ref.at[1 + direction],
            send_sem=cf_send.at[direction],
            recv_sem=cf_recv.at[direction],
            device_id=(g, t + (1 if direction else -1)),
            device_id_type=MESH,
        )

    def edge_copy(side, dt):
        rows = {-1: slice(0, 4), 0: slice(0, 8), 1: slice(4, 8)}[dt]
        return pltpu.make_async_remote_copy(
            src_ref=t_ref.at[rows],
            dst_ref=x_ref.at[side, 1 - dt, rows],
            send_sem=edge_send.at[side, 1 - dt],
            recv_sem=edge_recv.at[side, 1 - dt],
            device_id=(g + (1 if side else -1), t + dt),
            device_id_type=MESH,
        )

    lane = lanes_of()
    sub = lax.broadcasted_iota(jnp.int32, (8, LANES), 0)
    within = lane & 15
    shared = ((lane + EDGE) & 15) < 2 * EDGE
    cell_rows = cells_ref.reshape(2 * 2 * K * NYD, LANES)
    halo = 2 * K * NYD
    top, bottom = t == 0, t == tiles - 1

    def row_of(e):
        above = e < EDGE
        below = e >= EDGE + NYD
        where = jnp.where(above & ~top, 0, jnp.where(below & ~bottom, 2, 1))
        y = jnp.where(
            above,
            jnp.where(top, EDGE - 1 - e, e + NYD - EDGE),
            jnp.where(below & bottom, EDGE + 2 * NYD - 1 - e, e - EDGE - jnp.where(below, NYD, 0)),
        )
        return where, y

    row_at = [
        (1, e - EDGE) if EDGE <= e < EDGE + NYD else row_of(jnp.int32(e)) for e in range(EXT)
    ]

    def main_of(f, e, b):
        base = f * (K * NYD) + 64 * b
        where, y = row_at[e]
        if e < EDGE or e >= EDGE + NYD:
            base = base + jnp.where(where == 1, 0, halo)
        return cell_rows[pl.ds(base + y, 8, stride=NYD), :]

    def pack_coefs(e):
        where, y = row_at[e]
        source = 0 if isinstance(where, int) else jnp.where(where == 1, 0, 2 if e < EDGE else 1)
        rows = [jnp.broadcast_to(cf_ref[source, i, pl.ds(y, 1), :], (8, LANES)) for i in range(2)]
        block = jnp.where(sub == 0, rows[0], rows[1])
        block = jnp.where((lane < 8) | (lane >= LANES - 8), block, 0.0)
        for shift in (16, 32, 64):
            block = block + pltpu.roll(block, shift, 1)
        o_ref[e, COEF] = block
        own = rows[0]
        co_ref[0, 0, e] = (own + (1.0 - 4.0 * DIFFUSION)) * (1.0 / DIFFUSION)
        for s in range(1, STEPS + 1):
            co_ref[0, s, e] = rows[1] * ((1.0 - SLOW_RATE) ** (s - 1) / DIFFUSION**s)

    def send(c):
        for direction in range(2):
            @pl.when(has[1 if direction else -1])
            def _():
                for copy in row_copies(direction, c):
                    copy.start()

    def receive(c):
        for direction in range(2):
            @pl.when(has[-1 if direction else 1])
            def _():
                for copy in row_copies(direction, c):
                    copy.wait_recv()

    def settle(c):
        for direction in range(2):
            @pl.when(has[1 if direction else -1])
            def _():
                for copy in row_copies(direction, c):
                    copy.wait_send()

    for copy in cf_copies:
        copy.wait()
    wide_g = 1 + (g > 0).astype(jnp.int32) + (g < groups - 1).astype(jnp.int32)
    wide_t = 1 + (t > 0).astype(jnp.int32) + (t < tiles - 1).astype(jnp.int32)
    pl.semaphore_wait(barrier, wide_g * wide_t - 1 + len(greeted))

    for direction in range(2):
        @pl.when(has[1 if direction else -1])
        def _():
            cf_copy(direction).start()
    for group in range(GROUPS_K):
        local_copy(group).wait()
        for c in range(2 * group, min(2 * group + 2, WINDOW)):
            send(c)
    for y in range(NYD):
        pack_coefs(EDGE + y)
    for group in range(GROUPS_K):
        def pack_row(y, _):
            for f in range(2):
                packed = None
                for m in range(8):
                    block = cell_rows[pl.ds(f * (K * NYD) + 64 * (8 * group + m) + y, 8, stride=NYD), :]
                    if m == 0:
                        packed = block
                    else:
                        packed = jnp.where(
                            (lane >= 16 * m - 8) & (lane < 16 * m + 8), pltpu.roll(block, 16 * m, 1), packed
                        )
                o_ref[EDGE + y, f * (GROUPS_K + 1) + group] = packed
            return 0

        lax.fori_loop(0, NYD, pack_row, 0)

    def share_row(y, _):
        for i, (one, two) in enumerate(PAIRS):
            value = o_ref[EDGE + y, one]
            if two is not None:
                value = jnp.where(shared, value, pltpu.roll(o_ref[EDGE + y, two], 8, 1))
            t_ref[y, i] = value
        return 0

    lax.fori_loop(0, NYD, share_row, 0)

    for dt in (0, -1, 1):
        for side in range(2):
            @pl.when(exists(1 if side else -1, dt))
            def _():
                edge_copy(side, dt).start()
    for direction in range(2):
        @pl.when(has[-1 if direction else 1])
        def _():
            cf_copy(direction).wait_recv()
    for e in range(EXT):
        if e < EDGE or e >= EDGE + NYD:
            pack_coefs(e)

    def evolve(loads, coefs, stores):
        lots = range(len(loads))
        fast = [[[None] * EXT for _ in range(STEPS + 1)] for _ in lots]
        slow = [[[None] * EXT for _ in range(STEPS + 1)] for _ in lots]
        for e in range(EXT):
            for n in lots:
                fast[n][0][e] = loads[n](0, e)
                if 1 <= e < EXT - 1:
                    slow[n][0][e] = loads[n](1, e)
            for s in range(1, STEPS + 1):
                r = e - s
                if r < s or r > EXT - 1 - s:
                    continue
                drift = SLOW_RATE * DIFFUSION ** (s - 1) / (1.0 - SLOW_RATE) ** s
                for n in lots:
                    before = fast[n][s - 1]
                    old, old_slow = before[r], slow[n][s - 1][r]
                    total = (before[r - 1] + before[r + 1]) + (
                        pltpu.roll(old, 1, 1) + pltpu.roll(old, LANES - 1, 1)
                    )
                    new = total + (coefs[n](0, r) * old + coefs[n](s, r) * old_slow)
                    new_slow = old_slow + drift * old
                    fast[n][s][r] = new
                    slow[n][s][r] = new_slow
                    if s == STEPS:
                        stores[n](r - EDGE, new * DIFFUSION**STEPS)
                        stores[n](NYD + r - EDGE, new_slow * (1.0 - SLOW_RATE) ** STEPS)

    def block_steps(first):
        loads, stores = [], []
        for n in range(TOGETHER):
            b = first + n
            group = b // 8
            m = b - 8 * group
            rows = pl.ds(pl.multiple_of(8 * b, 8), 8)
            here = ((lane + 8) & (LANES - 1)) // 16 == m

            def load(f, e, b=b, group=group, m=m, here=here):
                value = main_of(f, e, b)
                if e < EDGE or e >= EDGE + NYD:
                    slot = f * (GROUPS_K + 1) + group
                    o_ref[e, slot] = jnp.where(here, pltpu.roll(value, 16 * m, 1), o_ref[e, slot])
                return value

            def store(fy, value, rows=rows):
                e_ref[fy, rows, :] = value

            loads.append(load)
            stores.append(store)
        evolve(loads, [lambda s, r: co_ref[0, s, r]] * TOGETHER, stores)

    def chunk(c, _):
        receive(c)

        @pl.when(c < CHUNKS - WINDOW)
        def _():
            send(c + WINDOW)

        def step(i, _):
            block_steps(PER_CHUNK * c + TOGETHER * i)
            return 0

        lax.fori_loop(0, PER_CHUNK // TOGETHER, step, 0)
        return 0

    lax.fori_loop(0, CHUNKS, chunk, 0)

    for dt in (0, -1, 1):
        for side in range(2):
            @pl.when(exists(-1 if side else 1, -dt))
            def _():
                edge_copy(side, dt).wait_recv()

    def join(side, e, slot, value):
        beside = within < EDGE if side == 0 else within >= 16 - EDGE
        q_ref[side, e, slot] = jnp.where(beside, value, o_ref[e, slot])

    for side in range(2):
        @pl.when(hasg[-1 if side else 1])
        def _():
            def join_row(k, _):
                for e in (4 * k, 4 * k + 1, 4 * k + 2, 4 * k + 3):
                    where, y = row_of(e)
                    for i, (one, two) in enumerate(PAIRS):
                        value = x_ref[side, where, y, i]
                        join(side, e, one, value)
                        if two is not None:
                            join(side, e, two, pltpu.roll(value, LANES - 8, 1))
                return 0

            lax.fori_loop(0, EXT // 4, join_row, 0)

        @pl.when(g == (0 if side else groups - 1))
        def _():
            def mirror_row(k, _):
                for e in (4 * k, 4 * k + 1, 4 * k + 2, 4 * k + 3):
                    for slot in range(SLOTS):
                        value = o_ref[e, slot]
                        flipped = None
                        for i in range(EDGE):
                            shift = LANES - 7 + 2 * i if side else 1 + 2 * i
                            moved = pltpu.roll(value, shift, 1)
                            flipped = moved if flipped is None else jnp.where((lane & 3) == i, moved, flipped)
                        join(side, e, slot, flipped)
                return 0

            lax.fori_loop(0, EXT // 4, mirror_row, 0)

    def side_coefs(k, _):
        for side, e in [(side, 2 * k - 1 + i) for side in range(2) for i in range(2)]:
            packed = q_ref[side, e, COEF]
            own = jnp.broadcast_to(packed[0:1, :], (8, LANES))
            cross = jnp.broadcast_to(packed[1:2, :], (8, LANES))
            co_ref[1 + side, 0, e] = (own + (1.0 - 4.0 * DIFFUSION)) * (1.0 / DIFFUSION)
            for s in range(1, STEPS + 1):
                co_ref[1 + side, s, e] = cross * ((1.0 - SLOW_RATE) ** (s - 1) / DIFFUSION**s)
        return 0

    lax.fori_loop(1, EXT // 2, side_coefs, 0)

    def side_step(group, _):
        loads, coefs, stores = [], [], []
        for side in range(2):
            loads.append(lambda f, e, side=side: q_ref[side, e, f * (GROUPS_K + 1) + group])
            coefs.append(lambda s, r, side=side: co_ref[1 + side, s, r])

            def store(fy, value, side=side):
                out_ref[side, fy, group] = value

            stores.append(store)
        evolve(loads, coefs, stores)
        return 0

    lax.fori_loop(0, GROUPS_K, side_step, 0)

    at_side = (lane < EDGE) | (lane >= LANES - EDGE)

    def merge(i, _):
        for fy in (4 * i, 4 * i + 1, 4 * i + 2, 4 * i + 3):
            for group in range(GROUPS_K):
                value = jnp.where(within < 8, out_ref[1, fy, group], out_ref[0, fy, group])
                for m in range(8):
                    rows = slice(64 * group + 8 * m, 64 * group + 8 * m + 8)
                    moved = pltpu.roll(value, LANES - 16 * m, 1) if m else value
                    e_ref[fy, rows, :] = jnp.where(at_side, moved, e_ref[fy, rows, :])
        return 0

    lax.fori_loop(0, NYD // 2, merge, 0)

    def drain():
        def finish(c, _):
            settle(c)
            return 0

        lax.fori_loop(0, CHUNKS, finish, 0)
        for dt in (0, -1, 1):
            for side in range(2):
                @pl.when(exists(1 if side else -1, dt))
                def _():
                    edge_copy(side, dt).wait_send()
        for direction in range(2):
            @pl.when(has[1 if direction else -1])
            def _():
                cf_copy(direction).wait_send()

    return drain


def eliminate(w_ref, emit, invert):
    lane = lanes_of()
    sub = lax.broadcasted_iota(jnp.int32, (8, LANES), 0)
    panels = K // 8
    for p in range(panels):
        j0 = 8 * p
        h, l0 = j0 // LANES, j0 % LANES
        halves = (0, 1) if invert else tuple(range(h, 2))
        inside = (lane >= l0) & (lane < l0 + 8)
        blk = {v: w_ref[j0 : j0 + 8, LANES * v : LANES * v + LANES] for v in halves}
        cols = [jnp.broadcast_to(blk[h][:, l0 + i : l0 + i + 1], (8, LANES)) for i in range(8)]
        el = [
            [jnp.broadcast_to(cols[i][m : m + 1, :], (8, LANES)) if m >= i else None for i in range(8)]
            for m in range(8)
        ]
        if invert:
            blk[h] = jnp.where(inside, jnp.where(lane - l0 == sub, 1.0, 0.0), blk[h])
        rows = {v: [jnp.broadcast_to(blk[v][m : m + 1, :], (8, LANES)) for m in range(8)] for v in halves}
        fac = [[None] * 8 for _ in range(8)]
        r, r2, pivots = [], [], []
        for i in range(8):
            pivots.append(el[i][i])
            r.append(lax.rsqrt(el[i][i]))
            r2.append(r[i] * r[i])
            for m in range(i + 1, 8):
                fac[m][i] = el[m][i] * r2[i]
            for k in range(i + 1, 8):
                for m in range(k, 8):
                    el[m][k] = el[m][k] - fac[k][i] * el[m][i]
            for v in halves:
                for m in range(i + 1, 8):
                    rows[v][m] = rows[v][m] - fac[m][i] * rows[v][i]
        for v in halves:
            out = rows[v][0] * r[0]
            for i in range(1, 8):
                out = jnp.where(sub == i, rows[v][i] * r[i], out)
            emit(p, v, out, lane, sub)
        emit(p, None, pivots, lane, sub)
        if p == panels - 1:
            break
        z = {v: [None] * 8 for v in halves}
        for v in halves:
            for i in range(7, -1, -1):
                acc = rows[v][i] * r2[i]
                for m in range(7, i, -1):
                    acc = acc - fac[m][i] * z[v][m]
                z[v][i] = acc
        for s in range(p + 1, panels):
            rng = slice(8 * s, 8 * s + 8)
            src = w_ref[rng, LANES * h : LANES * h + LANES]
            low = [jnp.broadcast_to(src[:, l0 + i : l0 + i + 1], (8, LANES)) for i in range(8)]
            for v in halves:
                if v == h:
                    cur = jnp.where(inside, 0.0, src) if invert else src
                else:
                    cur = w_ref[rng, LANES * v : LANES * v + LANES]
                a = low[0] * z[v][0]
                b = low[1] * z[v][1]
                for i in range(2, 8, 2):
                    a = a + low[i] * z[v][i]
                    b = b + low[i + 1] * z[v][i + 1]
                w_ref[rng, LANES * v : LANES * v + LANES] = cur - (a + b)
        yield


def split(a):
    high = a.astype(jnp.bfloat16)
    rest = a - high.astype(F32)
    middle = rest.astype(jnp.bfloat16)
    return high, middle, (rest - middle.astype(F32)).astype(jnp.bfloat16)


def gram_of(e_ref):
    def product(a, b):
        return lax.dot_general(a, b, (((1,), (1,)), ((), ())), preferred_element_type=F32)

    same = jnp.zeros((K, K), F32)
    mixed = jnp.zeros((K, K), F32)
    for y in range(NYD):
        a = jnp.concatenate([e_ref[y], e_ref[NYD + y]], axis=1)
        high, middle, low = split(a)
        same = same + product(high, high) + product(middle, middle)
        mixed = mixed + product(high, middle) + product(high, low)
    return same + mixed + jnp.transpose(mixed)


def tail_part(
    groups, tiles, line,
    e_ref, o_ref, r_ref,
    p_ref, near_ref, y_ref, z_ref, w_ref, sends, recvs,
):
    q, g, z, piece, inner, outer, in_line, in_y, in_z = line
    gram = gram_of(e_ref)
    p_ref[0:64, :] = gram[0:64, 0:128]
    p_ref[64:128, :] = jnp.concatenate([gram[0:64, 128:192], gram[64:128, 64:128]], axis=1)
    p_ref[128:192, :] = jnp.concatenate([gram[64:128, 128:192], gram[128:192, 128:192]], axis=1)

    count = [0]

    def copy_to(src, dst, peer):
        i = count[0]
        count[0] += 1
        copy = pltpu.make_async_remote_copy(
            src_ref=src, dst_ref=dst, send_sem=sends.at[i], recv_sem=recvs.at[i],
            device_id=peer, device_id_type=MESH,
        )
        copy.start()
        return copy

    def rows(index):
        return pl.ds(pl.multiple_of(index * piece, 8), piece)

    def emit_factor(p, v, out, lane, sub):
        if v is None:
            return
        value = jnp.where(lane + LANES * v >= sub + 8 * p, out, 0.0)
        r_ref[8 * p : 8 * p + 8, LANES * v : LANES * v + LANES] = value

    local = eliminate(w_ref, emit_factor, False)

    def advance(panels):
        for _ in range(panels):
            next(local, None)

    started = []
    phase = []
    for d in range(1, inner):
        phase.append(copy_to(p_ref.at[rows(lax.rem(q + d, inner))], near_ref.at[d - 1], in_line(d)))
    w_ref[:, 0:LANES] = gram[:, 0:LANES]
    w_ref[:, LANES:K] = gram[:, LANES:K]
    w_ref[:, K : 2 * LANES] = jnp.zeros((K, 2 * LANES - K), F32)
    r_ref[...] = jnp.zeros_like(r_ref)
    advance(8)
    total = p_ref[rows(q), :]
    for d, copy in enumerate(phase):
        copy.wait_recv()
        total = total + near_ref[d]
    started += phase
    for buf, me, size, peer_of in ((y_ref, g, groups, in_y), (z_ref, z, outer, in_z)):
        buf[me] = total
        phase = [copy_to(buf.at[me], buf.at[me], peer_of(d)) for d in range(1, size)]
        advance(6)
        for copy in phase:
            copy.wait_recv()
        total = buf[0]
        for i in range(1, size):
            total = total + buf[i]
        started += phase
    o_ref[rows(q), :] = total
    phase = [copy_to(o_ref.at[rows(q)], o_ref.at[rows(q)], in_line(d)) for d in range(1, inner)]
    advance(K // 8)
    for copy in phase:
        copy.wait_recv()
    started += phase
    for copy in started:
        copy.wait_send()


def solve_kernel(scale, o_ref, r_ref, c_ref, growth_ref, v_ref, inv_ref):
    u0, u1, u2 = o_ref[0:64, :], o_ref[64:128, :], o_ref[128:192, :]
    t0, t1, t2 = jnp.transpose(u0), jnp.transpose(u1), jnp.transpose(u2)
    v_ref[0:64, 0:LANES] = u0
    v_ref[0:64, LANES:] = u1
    v_ref[64:128, 0:LANES] = jnp.concatenate([t0[64:128], u1[:, 64:128]], axis=1)
    v_ref[64:128, LANES:] = u2
    v_ref[128:192, 0:LANES] = jnp.concatenate([t1[0:64], t2[0:64]], axis=1)
    v_ref[128:192, LANES:] = pltpu.roll(u2, 64, 1)
    diagonal = [jnp.ones((8, LANES), F32), jnp.ones((8, LANES), F32)]

    def emit_inverse(p, v, out, lane, sub):
        if v is None:
            h, l0 = 8 * p // LANES, 8 * p % LANES
            for i in range(8):
                diagonal[h] = jnp.where(lane == l0 + i, out[i], diagonal[h])
            return
        value = jnp.where(lane + LANES * v <= sub + 8 * p, out, 0.0)
        inv_ref[8 * p : 8 * p + 8, LANES * v : LANES * v + LANES] = value

    for _ in eliminate(v_ref, emit_inverse, True):
        pass
    growth_ref[0:1, 0:LANES] = 0.5 * jnp.log(diagonal[0][0:1, :])
    growth_ref[0:1, LANES:K] = 0.5 * jnp.log(diagonal[1][0:1, 0 : K - LANES])
    c_ref[...] = scale * lax.dot_general(
        r_ref[...], inv_ref[...], (((1,), (1,)), ((), ())),
        precision=lax.Precision.HIGHEST, preferred_element_type=F32,
    )


def main_kernel(groups, tiles, tan_hbm, self_hbm, cross_hbm, reduced_ref, factor_ref, e_ref, *scratch):
    g = lax.axis_index("grp")
    t = lax.axis_index("tile")
    inner = 8
    outer = tiles // inner
    piece = K // inner
    z = t // inner
    q = t - z * inner

    def in_line(d):
        return (g, z * inner + lax.rem(q + d, inner))

    def in_y(d):
        return (lax.rem(g + d, groups), t)

    def in_z(d):
        return (g, lax.rem(z + d, outer) * inner + q)

    peers = (
        [in_line(d) for d in range(1, inner)]
        + [in_y(d) for d in range(1, groups)]
        + [in_z(d) for d in range(1, outer)]
    )
    line = (q, g, z, piece, inner, outer, in_line, in_y, in_z)
    front_scratch, tail_scratch = scratch[:16], scratch[16:]
    drain = front_part(groups, tiles, peers, tan_hbm, self_hbm, cross_hbm, e_ref, *front_scratch)
    tail_part(groups, tiles, line, e_ref, reduced_ref, factor_ref, *tail_scratch)
    drain()


def run_main(groups, tiles, *arguments):
    hbm = pl.BlockSpec(memory_space=pltpu.HBM)
    copies = 2 * 7 + (groups - 1) + (tiles // 8 - 1)
    return pl.pallas_call(
        functools.partial(main_kernel, groups, tiles),
        out_shape=(jax.ShapeDtypeStruct((K, LANES), F32), jax.ShapeDtypeStruct((K, 2 * LANES), F32)),
        in_specs=[hbm] * 3,
        out_specs=[VMEM_SPEC] * 2,
        scratch_shapes=[
            pltpu.VMEM((2 * NYD, K, LANES), F32),
            pltpu.VMEM((2, 2, K, NYD, LANES), F32),
            pltpu.VMEM((3, 2, NYD, LANES), F32),
            pltpu.VMEM((EXT, SLOTS, 8, LANES), F32),
            pltpu.VMEM((NYD, len(PAIRS), 8, LANES), F32),
            pltpu.VMEM((2, 3, NYD, len(PAIRS), 8, LANES), F32),
            pltpu.VMEM((2, EXT, SLOTS, 8, LANES), F32),
            pltpu.VMEM((2, 2 * NYD, GROUPS_K, 8, LANES), F32),
            pltpu.VMEM((3, STEPS + 1, EXT, 8, LANES), F32),
            pltpu.SemaphoreType.DMA((GROUPS_K,)),
            pltpu.SemaphoreType.DMA((2,)),
            pltpu.SemaphoreType.DMA((2,)),
            pltpu.SemaphoreType.DMA((2,)),
            pltpu.SemaphoreType.DMA((2, CHUNKS, 2)),
            pltpu.SemaphoreType.DMA((2, CHUNKS, 2)),
            pltpu.SemaphoreType.DMA((2, 3)),
            pltpu.SemaphoreType.DMA((2, 3)),
            pltpu.VMEM((K, LANES), F32),
            pltpu.VMEM((7, K // 8, LANES), F32),
            pltpu.VMEM((groups, K // 8, LANES), F32),
            pltpu.VMEM((tiles // 8, K // 8, LANES), F32),
            pltpu.VMEM((K, 2 * LANES), F32),
            pltpu.SemaphoreType.DMA((copies,)),
            pltpu.SemaphoreType.DMA((copies,)),
        ],
        compiler_params=pltpu.CompilerParams(
            collective_id=0, has_side_effects=True, vmem_limit_bytes=LIMIT
        ),
        name="main",
    )(*[pltpu.with_memory_space_constraint(x, pltpu.HBM) for x in arguments])


def solve(scale, reduced, local_factor):
    return pl.pallas_call(
        functools.partial(solve_kernel, scale),
        out_shape=(jax.ShapeDtypeStruct((K, K), F32), jax.ShapeDtypeStruct((1, K), F32)),
        in_specs=[VMEM_SPEC] * 2,
        out_specs=[VMEM_SPEC] * 2,
        scratch_shapes=[pltpu.VMEM((K, 2 * LANES), F32)] * 2,
        compiler_params=pltpu.CompilerParams(vmem_limit_bytes=LIMIT),
        name="solve",
    )(reduced, local_factor)


def per_device(groups, tiles, tangents, reaction_self, reaction_cross):
    reduced, local_factor = run_main(groups, tiles, tangents, reaction_self, reaction_cross)
    corrections, growth = solve(math.sqrt(groups * tiles), reduced, local_factor)
    return (corrections, growth.reshape(K))


def solution(mesh):
    groups, tiles = mesh.shape["grp"], mesh.shape["tile"]
    in_specs = (P(None, None, "tile", "grp"), P("tile", "grp"), P("tile", "grp"))
    out_specs = (P(("grp", "tile"), None), P())
    return jax.shard_map(
        functools.partial(per_device, groups, tiles),
        mesh=mesh, in_specs=in_specs, out_specs=out_specs, check_vma=False,
    )
```
